256 devices in a mesh: dp: 16 (over z, x_hi), pipe: 4 (over y), tensor: 4 (over x_lo, core).
Axes of the slice: x: 4 (x_hi: 2, x_lo: 2; x = x_hi * 2 + x_lo), y: 4, z: 8, core: 2. Of those that a mesh axis runs over, the one named last changes fastest.
Arguments:
- grad_out: bfloat16 [8, 1024, 4096], P(None, 'dp', 'tensor'), may hold values from -6 to 6
- activations: bfloat16 [4, 3, 8, 1024, 4096], P('pipe', None, None, 'dp', 'tensor'), may hold values from -6 to 6
- mixing: bfloat16 [4, 3, 32, 128, 128], P('pipe', None, 'tensor'), may hold values from -0.1875 to 0.1875
- proj_tiles: bfloat16 [4, 3, 8, 128, 128], P('pipe'), may hold values from -0.1875 to 0.1875
- proj_blocks: int32 [4, 3, 8], P('pipe'), may hold values from 0 to 31, all different within a row
- section_sizes: int32 [4], replicated, may hold values from 1 to 3, 8 in all
Outputs:
- segment_grads: bfloat16 [4, 8, 1024, 4096], P('pipe', None, 'dp', 'tensor')
- sketches: float32 [4, 3, 8, 4096], P('pipe')
The draws below stay inside these ranges and needn't reach their ends.
Inputs may be any that keep to these rules, and one draw needn't show every extreme that they name: `section_sizes`: each segment holds 1 to 3 layers, 8 in all, some segment exactly 3. `proj_blocks`: the 8 blocks of one slot are distinct.
All inputs are finite; a program needn't handle non-finite values.
Results may differ from the reference program's by a relative error of at most 0.0074.
Values may be sent and summed in bfloat16 or wider, within the bound.
A program may use at most 64 MiB of HBM per device.

```python
import math
import jax
import jax.numpy as jnp
import numpy as np
from jax import lax

D = 4096
HS = 128
RANK = 64
NP = 8
SLOTS = 3
MB = 8
HEADS = 32
MB_TOK = 1024
LAYERS = 8
N_PIPE = 4


def block_scale(own_key, dims, pieces, smallest, top_value):
    level = 1.0
    for position, shards_of in pieces:
        heights = jax.random.uniform(jax.random.fold_in(jax.random.fold_in(own_key, 6), position), (shards_of,), jnp.float32, smallest / len(pieces), top_value / len(pieces))
        level = level * jnp.repeat(jnp.exp(heights), dims[position] // shards_of).reshape((-1,) + (1,) * (len(dims) - 1 - position))
    return level


def different_ones(rng, rows, number_of, top, lift):
    order = jax.random.permutation(jax.random.fold_in(rng, 1), number_of)
    pull = order
    for power in range(3):
        pull = pull * pull // number_of
    pull = pull * lift // number_of
    chance = jax.random.randint(jax.random.fold_in(rng, 2), (rows, number_of), 0, 4096) + pull
    sure = jax.random.permutation(jax.random.fold_in(rng, 3), rows)[jnp.arange(number_of) % rows]
    chance = jnp.where(jnp.arange(rows)[:, None] == sure[None, :], 1 << 14, chance)
    priority = chance * number_of + jnp.arange(number_of)
    return lax.top_k(priority.astype(jnp.int32), top)[1].astype(jnp.int32)


def profile(count, total, limit, skew):
    portions = [(1 << 20) // math.isqrt(rank ** skew) + 1 for rank in range(2, count + 1)]
    rest, given = total - limit - (count - 1), [1] * (count - 1)
    while rest > 0:
        free = [i for i in range(count - 1) if given[i] < limit]
        pool, left = sum([portions[i] for i in free]), rest
        for i in free:
            addition = min(limit - given[i], max(1, left * portions[i] // pool), rest)
            given[i] = given[i] + addition
            rest = rest - addition
    return np.array([limit] + given)


def ragged_sizes(own_key, count, total, most, skew):
    if count == 2:
        one = jax.random.randint(own_key, (), max(1, total - most), min(most, total - 1) + 1)
        return jnp.stack([one, total - one])
    sizes = jnp.asarray(profile(count, total, most, skew), jnp.int32)
    twos = (count - 1) // 2
    donor, sink = sizes[1:1 + 2 * twos:2], sizes[2:2 + 2 * twos:2]
    margin = jnp.minimum(donor - 1, most - sink)
    passed = jax.random.randint(jax.random.fold_in(own_key, 1), (twos,), 0, 1 << 20) % (margin + 1)
    sizes = sizes.at[1:1 + 2 * twos:2].set(donor - passed).at[2:2 + 2 * twos:2].set(sink + passed)
    return sizes[jax.random.permutation(jax.random.fold_in(own_key, 2), count)]


def centred(rng, dims, width, bound, pieces=(), held_as=jnp.bfloat16):
    drawn = jax.random.normal(rng, dims, jnp.float32) * width
    if len(pieces) > 0:
        drawn = block_scale(rng, dims, pieces, -0.22, 0.18) * drawn
    return jnp.clip(drawn, min=-bound, max=bound).astype(held_as)


def setup_inputs(seed: int = 0) -> dict:
    seeds = jax.random.split(jax.random.key(seed), 7)
    return {
        "grad_out": centred(seeds[0], (MB, MB_TOK, D), 1.0, 6.0, ((1, 16), (2, 4))),
        "activations": centred(seeds[1], (N_PIPE, SLOTS, MB, MB_TOK, D), 1.0, 6.0, ((0, 4), (3, 16), (4, 4))),
        "mixing": centred(seeds[2], (N_PIPE, SLOTS, HEADS, HS, HS), (8 * HS) ** -0.5, 0.1875, ((0, 4), (2, 4))),
        "proj_tiles": centred(seeds[3], (N_PIPE, SLOTS, NP, HS, 2 * RANK), (NP * HS) ** -0.5, 0.1875, ((0, 4),)),
        "proj_blocks": different_ones(seeds[4], N_PIPE * SLOTS, D // HS, NP, 0).reshape((N_PIPE, SLOTS, NP)),
        "section_sizes": ragged_sizes(seeds[5], N_PIPE, LAYERS, SLOTS, 1).astype(jnp.int32),
    }


def silu_slope(value):
    sig = jax.nn.sigmoid(value)
    return sig * (1.0 + value * (1.0 - sig))

def reference(grad_out, activations, mixing, proj_tiles, proj_blocks, section_sizes):
    high = lax.Precision.HIGHEST
    scale = 1.0 / math.sqrt(MB_TOK)
    grad = grad_out
    segment_list = [None] * N_PIPE
    sketch_list = [None] * N_PIPE
    for segment in range(N_PIPE - 1, -1, -1):
        per_slot = [None] * SLOTS
        for slot in range(SLOTS - 1, -1, -1):
            live = slot < section_sizes[segment]
            heads_in = activations[segment, slot].reshape(MB, MB_TOK, HEADS, HS).astype(jnp.float32)
            weight = mixing[segment, slot].astype(jnp.float32)
            pre = jnp.einsum('mthc,hcd->mthd', heads_in, weight, precision=high)
            grad_heads = grad.reshape(MB, MB_TOK, HEADS, HS).astype(jnp.float32)
            delta = (grad_heads * silu_slope(pre)).astype(jnp.bfloat16)
            delta_wide = delta.astype(jnp.float32)
            back = jnp.einsum('mthd,hcd->mthc', delta_wide, weight, precision=high)
            moved = (grad_heads + back).reshape(MB, MB_TOK, D).astype(jnp.bfloat16)
            grad = jnp.where(live, moved, grad)
            blocks = proj_blocks[segment, slot].astype(jnp.int32)
            tiles = proj_tiles[segment, slot].astype(jnp.float32)
            picked_act = jnp.take(heads_in, blocks, axis=2)
            picked_delta = jnp.take(delta_wide, blocks, axis=2)
            act_proj = jnp.einsum('mtjc,jcr->mtr', picked_act, tiles[:, :, :RANK], precision=high)
            grad_proj = jnp.einsum('mtjc,jcr->mtr', picked_delta, tiles[:, :, RANK:], precision=high)
            sketch = jnp.einsum('mtr,mts->mrs', grad_proj, act_proj, precision=high) * scale
            per_slot[slot] = jnp.where(live, sketch.reshape(MB, RANK * RANK), jnp.zeros((MB, RANK * RANK), jnp.float32))
        segment_list[segment] = grad
        sketch_list[segment] = jnp.stack(per_slot)
    return (jnp.stack(segment_list), jnp.stack(sketch_list))
```

```python
import functools
import math

import jax
import jax.numpy as jnp
from jax import lax
from jax.experimental import pallas as pl
from jax.experimental.pallas import tpu as pltpu
from jax.sharding import PartitionSpec as P

MESH = pl.DeviceIdType.MESH
GROUPS = 2
BLOCK = 8


def silu_slope(value):
    half = jnp.tanh(0.5 * value) * 0.5
    sig = 0.5 + half
    return sig * (1.0 + value * (0.5 - half))


def kernel(
    n_dp, n_pipe, n_tensor, scale,
    sizes, blocks, grad_hbm, acts_hbm, mix_hbm, tiles_hbm,
    gout_hbm, sk_hbm,
    acts, gin, gout, mix, tiles, dense, slope, delta, parts, red, sums, rs, tile, sk,
    acts_sem, grad_sem, weight_sem, gout_sem, sk_sem,
    relay_send, relay_recv, part_send, part_recv,
    rs_send, rs_recv, dp_send, dp_recv, tn_send, tn_recv,
):
    slots, micro, tokens, width = acts.shape
    heads = mix.shape[1]
    hs = mix.shape[2]
    rank = tiles.shape[3] // 2
    rows = sums.shape[1]
    pieces = rows // BLOCK
    turns = micro // n_tensor
    dp = lax.axis_index("dp")
    pipe = lax.axis_index("pipe")
    tensor = lax.axis_index("tensor")
    top = pipe == n_pipe - 1
    live = sizes[pipe]

    def device(d, p, t):
        return {"dp": d, "pipe": p, "tensor": t}

    mix_load = pltpu.make_async_copy(mix_hbm, mix, weight_sem.at[0])
    tiles_load = pltpu.make_async_copy(tiles_hbm, tiles, weight_sem.at[1])

    def acts_load(m):
        return pltpu.make_async_copy(acts_hbm.at[:, m], acts.at[:, m], acts_sem.at[m])

    def grad_load(m):
        return pltpu.make_async_copy(grad_hbm.at[m], gin.at[m], grad_sem.at[m])

    mix_load.start()
    acts_load(0).start()

    @pl.when(top)
    def _():
        grad_load(0).start()

    tiles_load.start()

    barrier = pltpu.get_barrier_semaphore()

    def greet(d, p, t):
        pl.semaphore_signal(barrier, inc=1, device_id=device(d, p, t), device_id_type=MESH)

    @pl.when(pipe > 0)
    def _():
        greet(dp, pipe - 1, tensor)

    @pl.when(pipe < n_pipe - 1)
    def _():
        greet(dp, pipe + 1, tensor)

    def greet_tensor(o, c):
        greet(dp, pipe, lax.rem(tensor + o, n_tensor))
        return c

    def greet_dp(o, c):
        greet(lax.rem(dp + o, n_dp), pipe, tensor)
        return c

    lax.fori_loop(1, n_tensor, greet_tensor, 0)
    lax.fori_loop(1, n_dp, greet_dp, 0)

    def load_rest(m, c):
        acts_load(m).start()

        @pl.when(top)
        def _():
            grad_load(m).start()

        return c

    lax.fori_loop(1, micro, load_rest, 0)

    def slopes(m):
        acts_load(m).wait()
        for k in range(slots):
            for h in range(heads):
                cols = pl.ds(h * hs, hs)
                pre = jnp.dot(acts[k, m, :, cols], mix[k, h], preferred_element_type=jnp.float32)
                slope[k, :, cols] = silu_slope(pre)

    def relay(m, q):
        cols = pl.ds(q * (width // GROUPS), width // GROUPS)
        return pltpu.make_async_remote_copy(
            src_ref=gout.at[m, :, cols], dst_ref=gin.at[m, :, cols],
            send_sem=relay_send.at[m, q], recv_sem=relay_recv.at[m, q],
            device_id=device(dp, lax.rem(pipe + n_pipe - 1, n_pipe), tensor), device_id_type=MESH,
        )

    def part_copy(m):
        owner = lax.rem(m, n_tensor)
        turn = m // n_tensor
        source = lax.rem(tensor - owner + n_tensor + n_tensor - 1, n_tensor)
        return pltpu.make_async_remote_copy(
            src_ref=parts.at[m], dst_ref=red.at[turn, source],
            send_sem=part_send.at[m], recv_sem=part_recv.at[turn, source],
            device_id=device(dp, pipe, owner), device_id_type=MESH,
        )

    def chain(m):
        @pl.when(top)
        def _():
            grad_load(m).wait()

        for q in range(GROUPS):
            @pl.when(jnp.logical_not(top))
            def _():
                relay(m, q).wait_recv()

            for h in range(q * heads // GROUPS, (q + 1) * heads // GROUPS):
                cols = pl.ds(h * hs, hs)
                g = gin[m, :, cols].astype(jnp.float32)
                for k in range(slots - 1, -1, -1):
                    d = (g * slope[k, :, cols]).astype(jnp.bfloat16)
                    delta[k, :, cols] = d
                    back = lax.dot_general(
                        d, mix[k, h], (((1,), (1,)), ((), ())), preferred_element_type=jnp.float32
                    )
                    moved = (g + back).astype(jnp.bfloat16).astype(jnp.float32)
                    g = jnp.where(k < live, moved, g)
                gout[m, :, cols] = g.astype(jnp.bfloat16)

            @pl.when(pipe > 0)
            def _():
                relay(m, q).start()

        pltpu.make_async_copy(gout.at[m], gout_hbm.at[m], gout_sem.at[m]).start()

    lanes = lax.broadcasted_iota(jnp.int32, (tokens, 2 * rank), 1)
    low = lanes < rank

    def project(m):
        for k in range(slots):
            both = jnp.concatenate([acts[k, m], delta[k]], axis=0)
            out = jnp.dot(both, dense[k], preferred_element_type=jnp.float32)
            parts[m, k] = jnp.where(low, out[:tokens], out[tokens:]).astype(jnp.bfloat16)

        @pl.when(lax.rem(m, n_tensor) != tensor)
        def _():
            part_copy(m).start()

    mix_load.wait()
    slopes(0)

    tiles_load.wait()
    r_in = lax.broadcasted_iota(jnp.int32, (2 * rank, 2 * rank), 0)
    r_out = lax.broadcasted_iota(jnp.int32, (2 * rank, 2 * rank), 1)
    back_out = r_out - rank
    half = rank // 2
    from_row = jnp.where(
        r_out < rank, r_out,
        rank + jnp.where(back_out < half, 2 * back_out, 2 * (back_out - half) + 1),
    )
    shuffle = jnp.where(r_in == from_row, 1.0, 0.0).astype(jnp.bfloat16)
    for k in range(slots):
        for b in range(heads):
            wanted = tensor * heads + b
            pick = 0
            found = 0
            for j in range(tiles.shape[1]):
                hit = blocks[k * tiles.shape[1] + j] == wanted
                pick = jnp.where(hit, j, pick)
                found = jnp.where(hit, 1, found)
            block = jnp.dot(tiles[k, pick], shuffle, preferred_element_type=jnp.float32)
            dense[k, pl.ds(b * hs, hs), :] = jnp.where(found == 1, block, 0.0).astype(jnp.bfloat16)

    peers = (n_tensor - 1) + (n_dp - 1)

    @pl.when(jnp.logical_and(pipe > 0, pipe < n_pipe - 1))
    def _():
        pl.semaphore_wait(barrier, peers + 2)

    @pl.when(jnp.logical_or(pipe == 0, pipe == n_pipe - 1))
    def _():
        pl.semaphore_wait(barrier, peers + 1)

    def step(m, c):
        chain(m)
        project(m)

        @pl.when(m + 1 < micro)
        def _():
            slopes(m + 1)

        return c

    lax.fori_loop(0, micro, step, 0)

    def piece_of(d):
        return lax.rem(d - 4 * tensor + 4 * n_dp, n_dp)

    def rs_copy(turn, peer, r, slot):
        return pltpu.make_async_remote_copy(
            src_ref=sums.at[turn, pl.ds(r * BLOCK, BLOCK)], dst_ref=rs.at[turn, slot],
            send_sem=rs_send.at[turn, slot], recv_sem=rs_recv.at[turn, slot],
            device_id=device(peer, pipe, tensor), device_id_type=MESH,
        )

    def dp_copy(turn, m, peer, r, slot):
        return pltpu.make_async_remote_copy(
            src_ref=tile.at[turn], dst_ref=sk.at[m, pl.ds(r * BLOCK, BLOCK)],
            send_sem=dp_send.at[turn, slot], recv_sem=dp_recv.at[turn, r],
            device_id=device(peer, pipe, tensor), device_id_type=MESH,
        )

    def tensor_copy(turn, m, o):
        return pltpu.make_async_remote_copy(
            src_ref=sk.at[m], dst_ref=sk.at[m],
            send_sem=tn_send.at[turn, o - 1], recv_sem=tn_recv.at[turn, o - 1],
            device_id=device(dp, pipe, lax.rem(tensor + o, n_tensor)), device_id_type=MESH,
        )

    mine = piece_of(dp)
    packed = lax.broadcasted_iota(jnp.int32, (rank // 2, 2 * rank), 1) < rank
    for turn in range(turns):
        m = turn * n_tensor + tensor
        for s in range(n_tensor - 1):
            pltpu.make_async_copy(red.at[turn, s], red.at[turn, s], part_recv.at[turn, s]).wait()
        for k in range(slots):
            x = parts[m, k].astype(jnp.float32)
            for s in range(n_tensor - 1):
                x = x + red[turn, s, k].astype(jnp.float32)
            y = jnp.where(low, x, pltpu.roll(x, rank, 1))
            t = lax.dot_general(
                x, y, (((0,), (0,)), ((), ())), precision=lax.Precision.HIGHEST,
                preferred_element_type=jnp.float32,
            )
            out = jnp.where(packed, t[rank : rank + half], t[rank + half :]) * scale
            sums[turn, pl.ds(k * (rank // 2), rank // 2), :] = jnp.where(k < live, out, 0.0)

        def scatter(o, c):
            peer = lax.rem(dp + o, n_dp)
            r = piece_of(peer)

            @pl.when(r < pieces)
            def _():
                rs_copy(turn, peer, r, o).start()

            return c

        lax.fori_loop(1, n_dp, scatter, 0)

    for turn in range(turns):
        m = turn * n_tensor + tensor

        @pl.when(mine < pieces)
        def _():
            def arrive(o, c):
                pltpu.make_async_copy(rs.at[turn, o], rs.at[turn, o], rs_recv.at[turn, o]).wait()
                return c

            lax.fori_loop(1, n_dp, arrive, 0)
            total = sums[turn, pl.ds(mine * BLOCK, BLOCK), :]
            for o in range(1, n_dp):
                total = total + rs[turn, o]
            tile[turn] = total
            sk[m, pl.ds(mine * BLOCK, BLOCK), :] = total

            def spread(o, c):
                dp_copy(turn, m, lax.rem(dp + o, n_dp), mine, o).start()
                return c

            lax.fori_loop(1, n_dp, spread, 0)

    for turn in range(turns):
        m = turn * n_tensor + tensor

        def collect(r, c):
            @pl.when(r != mine)
            def _():
                pltpu.make_async_copy(tile.at[turn], tile.at[turn], dp_recv.at[turn, r]).wait()

            return c

        lax.fori_loop(0, pieces, collect, 0)
        for o in range(1, n_tensor):
            tensor_copy(turn, m, o).start()

    for turn in range(turns):
        for o in range(1, n_tensor):
            pltpu.make_async_copy(sk.at[0], sk.at[0], tn_recv.at[turn, o - 1]).wait()
    out_copy = pltpu.make_async_copy(sk, sk_hbm, sk_sem)
    out_copy.start()

    def drain(m, c):
        @pl.when(pipe > 0)
        def _():
            for q in range(GROUPS):
                relay(m, q).wait_send()

        @pl.when(lax.rem(m, n_tensor) != tensor)
        def _():
            part_copy(m).wait_send()

        pltpu.make_async_copy(gout.at[m], gout_hbm.at[m], gout_sem.at[m]).wait()
        return c

    lax.fori_loop(0, micro, drain, 0)
    for turn in range(turns):
        m = turn * n_tensor + tensor

        def drain_rs(o, c):
            peer = lax.rem(dp + o, n_dp)
            r = piece_of(peer)

            @pl.when(r < pieces)
            def _():
                rs_copy(turn, peer, r, o).wait_send()

            @pl.when(mine < pieces)
            def _():
                dp_copy(turn, m, peer, mine, o).wait_send()

            return c

        lax.fori_loop(1, n_dp, drain_rs, 0)
        for o in range(1, n_tensor):
            tensor_copy(turn, m, o).wait_send()
    out_copy.wait()


def shards(n_dp, n_pipe, n_tensor, grad_out, activations, mixing, proj_tiles, proj_blocks, section_sizes):
    micro, tokens, width = grad_out.shape
    slots = activations.shape[1]
    heads, hs = mixing.shape[2:4]
    n_tiles = proj_tiles.shape[2]
    rank = proj_tiles.shape[4] // 2
    rows = slots * rank // 2
    turns = micro // n_tensor
    pieces = rows // BLOCK
    bf16, f32 = jnp.bfloat16, jnp.float32
    anywhere = pl.BlockSpec(memory_space=pl.ANY)
    smem = pl.BlockSpec(memory_space=pltpu.SMEM)
    dma = pltpu.SemaphoreType.DMA
    gout, sk = pl.pallas_call(
        functools.partial(kernel, n_dp, n_pipe, n_tensor, 1.0 / math.sqrt(tokens * n_dp)),
        out_shape=(
            jax.ShapeDtypeStruct((micro, tokens, width), bf16),
            jax.ShapeDtypeStruct((micro, rows, 2 * rank), f32),
        ),
        in_specs=[smem, smem, anywhere, anywhere, anywhere, anywhere],
        out_specs=(anywhere, anywhere),
        scratch_shapes=[
            pltpu.VMEM((slots, micro, tokens, width), bf16),
            pltpu.VMEM((micro, tokens, width), bf16),
            pltpu.VMEM((micro, tokens, width), bf16),
            pltpu.VMEM((slots, heads, hs, hs), bf16),
            pltpu.VMEM((slots, n_tiles, hs, 2 * rank), bf16),
            pltpu.VMEM((slots, width, 2 * rank), bf16),
            pltpu.VMEM((slots, tokens, width), f32),
            pltpu.VMEM((slots, tokens, width), bf16),
            pltpu.VMEM((micro, slots, tokens, 2 * rank), bf16),
            pltpu.VMEM((turns, n_tensor - 1, slots, tokens, 2 * rank), bf16),
            pltpu.VMEM((turns, rows, 2 * rank), f32),
            pltpu.VMEM((turns, n_dp, BLOCK, 2 * rank), f32),
            pltpu.VMEM((turns, BLOCK, 2 * rank), f32),
            pltpu.VMEM((micro, rows, 2 * rank), f32),
            dma((micro,)), dma((micro,)), dma((2,)), dma((micro,)), dma,
            dma((micro, GROUPS)), dma((micro, GROUPS)),
            dma((micro,)), dma((turns, n_tensor - 1)),
            dma((turns, n_dp)), dma((turns, n_dp)),
            dma((turns, n_dp)), dma((turns, pieces)),
            dma((turns, n_tensor - 1)), dma((turns, n_tensor - 1)),
        ],
        compiler_params=pltpu.CompilerParams(
            collective_id=0, has_side_effects=True, vmem_limit_bytes=48 << 20
        ),
    )(
        section_sizes, proj_blocks[0].reshape(-1), grad_out, activations[0], mixing[0], proj_tiles[0],
    )
    sk = sk.reshape(micro, slots, rank // 2, 2 * rank).transpose(1, 0, 2, 3)
    return gout[None], sk.reshape(1, slots, micro, rank * rank)


def solution(mesh):
    return jax.shard_map(
        functools.partial(shards, mesh.shape["dp"], mesh.shape["pipe"], mesh.shape["tensor"]),
        mesh=mesh,
        in_specs=(
            P(None, "dp", "tensor"),
            P("pipe", None, None, "dp", "tensor"),
            P("pipe", None, "tensor", None, None),
            P("pipe", None, None, None, None),
            P("pipe", None, None),
            P(),
        ),
        out_specs=(P("pipe", None, "dp", "tensor"), P("pipe", None, None, None)),
        check_vma=False,
    )
```

```python
import functools
import math

import jax
import jax.numpy as jnp
from jax import lax
from jax.experimental import pallas as pl
from jax.experimental.pallas import tpu as pltpu
from jax.sharding import PartitionSpec as P

MESH = pl.DeviceIdType.MESH
GROUPS = 2


def silu_slope(value):
    half = jnp.tanh(0.5 * value) * 0.5
    sig = 0.5 + half
    return sig * (1.0 + value * (0.5 - half))


def kernel(
    n_dp, n_pipe, n_tensor, scale,
    sizes, blocks, grad_hbm, acts_hbm, mix_hbm, tiles_hbm,
    gout, sk_out,
    acts, gin, mix, tiles, dense, slope, delta, parts, red, zbuf, sk, wide,
    acts_sem, grad_sem, weight_sem,
    relay_send, relay_recv, part_send, part_recv, z_send, z_recv, x_send, x_recv,
):
    slots, micro, tokens, width = acts.shape
    heads = mix.shape[1]
    hs = mix.shape[2]
    n_tiles = tiles.shape[1]
    rank = tiles.shape[3] // 2
    half = rank // 2
    ring = 2 * n_tensor
    n_z = n_dp // 2
    rounds = zbuf.shape[0]
    dp = lax.axis_index("dp")
    pipe = lax.axis_index("pipe")
    tensor = lax.axis_index("tensor")
    z = dp // 2
    side = lax.rem(dp, 2)
    me = side * n_tensor + tensor
    top = pipe == n_pipe - 1
    live = sizes[pipe]

    def at(zz, u, p=None):
        return {
            "dp": zz * 2 + u // n_tensor,
            "pipe": pipe if p is None else p,
            "tensor": lax.rem(u, n_tensor),
        }

    mix_load = pltpu.make_async_copy(mix_hbm.at[0], mix, weight_sem.at[0])
    tiles_load = pltpu.make_async_copy(tiles_hbm.at[0], tiles, weight_sem.at[1])

    def acts_load(m):
        return pltpu.make_async_copy(acts_hbm.at[0, :, m], acts.at[:, m], acts_sem.at[m])

    def grad_load(m):
        return pltpu.make_async_copy(grad_hbm.at[m], gin.at[m], grad_sem.at[m])

    mix_load.start()
    acts_load(0).start()

    @pl.when(top)
    def _():
        grad_load(0).start()

    barrier = pltpu.get_barrier_semaphore()

    def greet(where):
        pl.semaphore_signal(barrier, inc=1, device_id=where, device_id_type=MESH)

    @pl.when(pipe < n_pipe - 1)
    def _():
        greet(at(z, me, pipe + 1))

    @pl.when(pipe > 0)
    def _():
        greet(at(z, me, pipe - 1))

    for o in range(1, n_z):
        greet(at(lax.rem(z + o, n_z), me))
    for o in range(1, ring):
        greet(at(z, lax.rem(me + o, ring)))
    tiles_load.start()

    def load_rest(m, c):
        acts_load(m).start()

        @pl.when(top)
        def _():
            grad_load(m).start()

        return c

    lax.fori_loop(1, micro, load_rest, 0)

    def slopes(m):
        acts_load(m).wait()
        for h in range(heads):
            cols = pl.ds(h * hs, hs)
            for k in range(slots):
                pre = jnp.dot(acts[k, m, :, cols], mix[k, h], preferred_element_type=jnp.float32)
                slope[k, :, cols] = silu_slope(pre)

    def relay(m, q):
        cols = pl.ds(q * (width // GROUPS), width // GROUPS)
        return pltpu.make_async_remote_copy(
            src_ref=gout.at[m, :, cols], dst_ref=gin.at[m, :, cols],
            send_sem=relay_send.at[m, q], recv_sem=relay_recv.at[m, q],
            device_id=at(z, me, lax.rem(pipe + n_pipe - 1, n_pipe)), device_id_type=MESH,
        )

    def part_copy(m, k):
        n = m * slots + k
        owner = lax.rem(n, ring)
        turn = n // ring
        gap = lax.rem(tensor - lax.rem(owner, n_tensor) + n_tensor, n_tensor)
        slot = jnp.where(owner // n_tensor == side, gap - 1, n_tensor - 1 + gap)
        slot = jnp.maximum(slot, 0)
        return owner, pltpu.make_async_remote_copy(
            src_ref=parts.at[n], dst_ref=red.at[turn, slot],
            send_sem=part_send.at[n], recv_sem=part_recv.at[turn, slot],
            device_id=at(z, owner), device_id_type=MESH,
        )

    def chain(m):
        @pl.when(top)
        def _():
            grad_load(m).wait()

        for q in range(GROUPS):
            @pl.when(jnp.logical_not(top))
            def _():
                relay(m, q).wait_recv()

            for h in range(q * heads // GROUPS, (q + 1) * heads // GROUPS):
                cols = pl.ds(h * hs, hs)
                g = gin[m, :, cols].astype(jnp.float32)
                for k in range(slots - 1, -1, -1):
                    d = (g * slope[k, :, cols]).astype(jnp.bfloat16)
                    delta[k, :, cols] = d
                    back = lax.dot_general(
                        d, mix[k, h], (((1,), (1,)), ((), ())), preferred_element_type=jnp.float32
                    )
                    moved = (g + back).astype(jnp.bfloat16).astype(jnp.float32)
                    g = jnp.where(k < live, moved, g)
                gout[m, :, cols] = g.astype(jnp.bfloat16)

            @pl.when(pipe > 0)
            def _():
                relay(m, q).start()

    def low(size):
        return lax.broadcasted_iota(jnp.int32, (size, 2 * rank), 1) < rank

    def project(m):
        for k in range(slots - 1, -1, -1):
            both = jnp.concatenate([acts[k, m], delta[k]], axis=0)
            out = jnp.dot(both, dense[k], preferred_element_type=jnp.float32)
            parts[m * slots + k] = jnp.where(
                low(tokens), out[:tokens], out[tokens:]
            ).astype(jnp.bfloat16)
            owner, copy = part_copy(m, k)

            @pl.when(owner != me)
            def _():
                copy.start()

    def build():
        tiles_load.wait()
        r_in = lax.broadcasted_iota(jnp.int32, (2 * rank, 2 * rank), 0)
        r_out = lax.broadcasted_iota(jnp.int32, (2 * rank, 2 * rank), 1)
        moved = r_out - rank
        from_row = jnp.where(
            r_out < rank, r_out,
            rank + jnp.where(moved < half, 2 * moved, 2 * (moved - half) + 1),
        )
        shuffle = jnp.where(r_in == from_row, 1.0, 0.0).astype(jnp.bfloat16)
        for k in range(slots):
            for b in range(heads):
                wanted = tensor * heads + b
                pick = 0
                found = 0
                for j in range(n_tiles):
                    hit = blocks[k, 0, j] == wanted
                    pick = jnp.where(hit, j, pick)
                    found = jnp.where(hit, 1, found)
                block = jnp.dot(tiles[k, pick], shuffle, preferred_element_type=jnp.float32)
                dense[k, pl.ds(b * hs, hs), :] = jnp.where(found == 1, block, 0.0).astype(jnp.bfloat16)

    def z_copy(r, o):
        return pltpu.make_async_remote_copy(
            src_ref=zbuf.at[r, z], dst_ref=zbuf.at[r, z],
            send_sem=z_send.at[r, o - 1], recv_sem=z_recv.at[r, o - 1],
            device_id=at(lax.rem(z + o, n_z), me), device_id_type=MESH,
        )

    def x_copy(r, o):
        n = r * ring + me
        return pltpu.make_async_remote_copy(
            src_ref=sk.at[n], dst_ref=sk.at[n],
            send_sem=x_send.at[r, o - 1], recv_sem=x_recv.at[r, o - 1],
            device_id=at(z, lax.rem(me + o, ring)), device_id_type=MESH,
        )

    def outer(r):
        n = r * ring + me
        for s in range(ring - 1):
            pltpu.make_async_copy(red.at[r, s], red.at[r, s], part_recv.at[r, s]).wait()
        near = parts[n].astype(jnp.float32)
        for s in range(n_tensor - 1):
            near = near + red[r, s].astype(jnp.float32)
        far = red[r, n_tensor - 1].astype(jnp.float32)
        for s in range(n_tensor, ring - 1):
            far = far + red[r, s].astype(jnp.float32)
        x = jnp.concatenate([near, far], axis=0)
        y = jnp.where(low(2 * tokens), x, pltpu.roll(x, rank, 1))
        t = lax.dot_general(
            x, y, (((0,), (0,)), ((), ())), precision=lax.Precision.HIGHEST,
            preferred_element_type=jnp.float32,
        )
        out = jnp.where(low(half), t[rank : rank + half], t[rank + half :]) * scale
        zbuf[r, z] = jnp.where(lax.rem(n, slots) < live, out, 0.0).astype(jnp.bfloat16)
        for o in range(1, n_z):
            z_copy(r, o).start()

    def finish(r):
        for o in range(1, n_z):
            z_copy(r, o).wait_recv()
        total = zbuf[r, 0].astype(jnp.float32)
        for zz in range(1, n_z):
            total = total + zbuf[r, zz].astype(jnp.float32)
        sk[r * ring + me] = total.astype(jnp.bfloat16)
        for o in range(1, ring):
            x_copy(r, o).start()

    mix_load.wait()
    slopes(0)
    greeted = (n_z - 1) + (ring - 1)

    @pl.when(jnp.logical_and(pipe > 0, pipe < n_pipe - 1))
    def _():
        pl.semaphore_wait(barrier, greeted + 2)

    @pl.when(jnp.logical_or(pipe == 0, pipe == n_pipe - 1))
    def _():
        pl.semaphore_wait(barrier, greeted + 1)

    def step(m, c):
        chain(m)

        @pl.when(m == 0)
        def _():
            build()

        project(m)

        @pl.when(m + 1 < micro)
        def _():
            slopes(m + 1)

        for r in range(rounds - 1):
            @pl.when(m == (ring * (r + 1) - 1) // slots + 2)
            def _():
                outer(r)

        for r in range(rounds - 2):
            @pl.when(m == (ring * (r + 1) - 1) // slots + 4)
            def _():
                finish(r)

        return c

    lax.fori_loop(0, micro, step, 0)
    outer(rounds - 1)
    finish(rounds - 2)
    finish(rounds - 1)

    for r in range(rounds):
        for o in range(1, ring):
            x_copy(r, o).wait_recv()
    for n in range(slots * micro):
        wide[pl.ds(n * half, half), :] = sk[n].astype(jnp.float32)
    for k in range(slots):
        for i in range(half):
            sk_out[0, k, :, pl.ds(i * 2 * rank, 2 * rank)] = wide[
                pl.ds(k * half + i, micro, stride=slots * half), :
            ]

    def drain(m, c):
        @pl.when(pipe > 0)
        def _():
            for q in range(GROUPS):
                relay(m, q).wait_send()

        for k in range(slots):
            owner, copy = part_copy(m, k)

            @pl.when(owner != me)
            def _():
                copy.wait_send()

        return c

    lax.fori_loop(0, micro, drain, 0)
    for r in range(rounds):
        for o in range(1, n_z):
            z_copy(r, o).wait_send()
        for o in range(1, ring):
            x_copy(r, o).wait_send()


def shards(n_dp, n_pipe, n_tensor, grad_out, activations, mixing, proj_tiles, proj_blocks, section_sizes):
    micro, tokens, width = grad_out.shape
    slots = activations.shape[1]
    heads, hs = mixing.shape[2:4]
    n_tiles = proj_tiles.shape[2]
    rank = proj_tiles.shape[4] // 2
    units = micro * slots
    ring = 2 * n_tensor
    rounds = units // ring
    n_z = n_dp // 2
    bf16, f32 = jnp.bfloat16, jnp.float32
    hbm = pl.BlockSpec(memory_space=pltpu.HBM)
    vmem = pl.BlockSpec(memory_space=pltpu.VMEM)
    smem = pl.BlockSpec(memory_space=pltpu.SMEM)
    dma = pltpu.SemaphoreType.DMA
    gout, sk = pl.pallas_call(
        functools.partial(kernel, n_dp, n_pipe, n_tensor, 1.0 / math.sqrt(tokens * n_dp)),
        out_shape=(
            jax.ShapeDtypeStruct((micro, tokens, width), bf16),
            jax.ShapeDtypeStruct((1, slots, micro, rank * rank), f32),
        ),
        in_specs=[smem, smem, hbm, hbm, hbm, hbm],
        out_specs=(vmem, vmem),
        scratch_shapes=[
            pltpu.VMEM((slots, micro, tokens, width), bf16),
            pltpu.VMEM((micro, tokens, width), bf16),
            pltpu.VMEM((slots, heads, hs, hs), bf16),
            pltpu.VMEM((slots, n_tiles, hs, 2 * rank), bf16),
            pltpu.VMEM((slots, width, 2 * rank), bf16),
            pltpu.VMEM((slots, tokens, width), f32),
            pltpu.VMEM((slots, tokens, width), bf16),
            pltpu.VMEM((units, tokens, 2 * rank), bf16),
            pltpu.VMEM((rounds, ring - 1, tokens, 2 * rank), bf16),
            pltpu.VMEM((rounds, n_z, rank // 2, 2 * rank), bf16),
            pltpu.VMEM((units, rank // 2, 2 * rank), bf16),
            pltpu.VMEM((units * rank // 2, 2 * rank), f32),
            dma((micro,)), dma((micro,)), dma((2,)),
            dma((micro, GROUPS)), dma((micro, GROUPS)),
            dma((units,)), dma((rounds, ring - 1)),
            dma((rounds, n_z - 1)), dma((rounds, n_z - 1)),
            dma((rounds, ring - 1)), dma((rounds, ring - 1)),
        ],
        compiler_params=pltpu.CompilerParams(
            collective_id=0, has_side_effects=True, vmem_limit_bytes=67_043_328
        ),
    )(section_sizes, proj_blocks.transpose(1, 0, 2), grad_out, activations, mixing, proj_tiles)
    return gout[None], sk


def solution(mesh):
    return jax.shard_map(
        functools.partial(shards, mesh.shape["dp"], mesh.shape["pipe"], mesh.shape["tensor"]),
        mesh=mesh,
        in_specs=(
            P(None, "dp", "tensor"),
            P("pipe", None, None, "dp", "tensor"),
            P("pipe", None, "tensor", None, None),
            P("pipe", None, None, None, None),
            P("pipe", None, None),
            P(),
        ),
        out_specs=(P("pipe", None, "dp", "tensor"), P("pipe", None, None, None)),
        check_vma=False,
    )
```

```python
import functools
import math

import jax
import jax.numpy as jnp
from jax import lax
from jax.experimental import pallas as pl
from jax.experimental.pallas import tpu as pltpu
from jax.sharding import PartitionSpec as P

MESH = pl.DeviceIdType.MESH
GROUPS = 2


def silu_slope(value):
    half = jnp.tanh(0.5 * value) * 0.5
    sig = 0.5 + half
    return sig * (1.0 + value * (0.5 - half))


def store(gout, sk, gout_hbm, sk_hbm, sem):
    copies = [
        pltpu.make_async_copy(gout, gout_hbm.at[0], sem.at[0]),
        pltpu.make_async_copy(sk, sk_hbm, sem.at[1]),
    ]
    for copy in copies:
        copy.start()
    for copy in copies:
        copy.wait()


def kernel(
    n_dp, n_pipe, n_tensor, scale,
    sizes, blocks, grad_hbm, acts_hbm, mix_hbm, tiles_hbm,
    gout, sk_out,
    acts, gin, mix, tiles, dense, slope, delta, parts, red, zbuf, sk, wide,
    acts_sem, grad_sem, weight_sem,
    relay_send, relay_recv, part_send, part_recv, z_send, z_recv, x_send, x_recv,
):
    slots, micro, tokens, width = acts.shape
    heads = mix.shape[1]
    hs = mix.shape[2]
    n_tiles = tiles.shape[1]
    rank = tiles.shape[3] // 2
    half = rank // 2
    ring = 2 * n_tensor
    n_z = n_dp // 2
    rounds = zbuf.shape[0]
    dp = lax.axis_index("dp")
    pipe = lax.axis_index("pipe")
    tensor = lax.axis_index("tensor")
    z = dp // 2
    side = lax.rem(dp, 2)
    me = side * n_tensor + tensor
    top = pipe == n_pipe - 1
    live = sizes[pipe]

    def at(zz, u, p=None):
        return {
            "dp": zz * 2 + u // n_tensor,
            "pipe": pipe if p is None else p,
            "tensor": lax.rem(u, n_tensor),
        }

    mix_load = pltpu.make_async_copy(mix_hbm.at[0], mix, weight_sem.at[0])
    tiles_load = pltpu.make_async_copy(tiles_hbm.at[0], tiles, weight_sem.at[1])

    def acts_load(m):
        return pltpu.make_async_copy(acts_hbm.at[0, :, m], acts.at[:, m], acts_sem.at[m])

    def grad_load(m):
        return pltpu.make_async_copy(grad_hbm.at[m], gin.at[m], grad_sem.at[m])

    mix_load.start()
    acts_load(0).start()

    @pl.when(top)
    def _():
        grad_load(0).start()

    barrier = pltpu.get_barrier_semaphore()

    def greet(where):
        pl.semaphore_signal(barrier, inc=1, device_id=where, device_id_type=MESH)

    @pl.when(pipe < n_pipe - 1)
    def _():
        greet(at(z, me, pipe + 1))

    @pl.when(pipe > 0)
    def _():
        greet(at(z, me, pipe - 1))

    for o in range(1, n_z):
        greet(at(lax.rem(z + o, n_z), me))
    for o in range(1, ring):
        greet(at(z, lax.rem(me + o, ring)))
    tiles_load.start()

    def load_rest(m, c):
        acts_load(m).start()

        @pl.when(top)
        def _():
            grad_load(m).start()

        return c

    lax.fori_loop(1, micro, load_rest, 0)

    def slopes(m, k, h):
        cols = pl.ds(h * hs, hs)
        pre = jnp.dot(acts[k, m, :, cols], mix[k, h], preferred_element_type=jnp.float32)
        slope[k, :, cols] = silu_slope(pre)

    def relay(m, q):
        cols = pl.ds(q * (width // GROUPS), width // GROUPS)
        return pltpu.make_async_remote_copy(
            src_ref=gout.at[m, :, cols], dst_ref=gin.at[m, :, cols],
            send_sem=relay_send.at[m, q], recv_sem=relay_recv.at[m, q],
            device_id=at(z, me, lax.rem(pipe + n_pipe - 1, n_pipe)), device_id_type=MESH,
        )

    def part_copy(m, k):
        n = m * slots + k
        owner = lax.rem(n, ring)
        turn = n // ring
        gap = lax.rem(tensor - lax.rem(owner, n_tensor) + n_tensor, n_tensor)
        slot = jnp.where(owner // n_tensor == side, gap - 1, n_tensor - 1 + gap)
        slot = jnp.maximum(slot, 0)
        return owner, pltpu.make_async_remote_copy(
            src_ref=parts.at[n], dst_ref=red.at[turn, slot],
            send_sem=part_send.at[n], recv_sem=part_recv.at[turn, slot],
            device_id=at(z, owner), device_id_type=MESH,
        )

    def chain(m):
        after = jnp.minimum(m + 1, micro - 1)

        @pl.when(top)
        def _():
            grad_load(m).wait()

        @pl.when(m + 1 < micro)
        def _():
            acts_load(after).wait()

        for q in range(GROUPS):
            @pl.when(jnp.logical_not(top))
            def _():
                relay(m, q).wait_recv()

            some = range(q * heads // GROUPS, (q + 1) * heads // GROUPS)
            g = {h: gin[m, :, pl.ds(h * hs, hs)] for h in some}
            for k in range(slots - 1, -1, -1):
                back = {}
                for h in some:
                    cols = pl.ds(h * hs, hs)
                    d = (g[h].astype(jnp.float32) * slope[k, :, cols]).astype(jnp.bfloat16)
                    delta[k, :, cols] = d
                    back[h] = lax.dot_general(
                        d, mix[k, h], (((1,), (1,)), ((), ())), preferred_element_type=jnp.float32
                    )
                for h in some:
                    slopes(after, k, h)
                for h in some:
                    moved = (g[h].astype(jnp.float32) + back[h]).astype(jnp.bfloat16)
                    g[h] = jnp.where(k < live, moved, g[h])
            for h in some:
                gout[m, :, pl.ds(h * hs, hs)] = g[h]

            @pl.when(pipe > 0)
            def _():
                relay(m, q).start()

    def low(size):
        return lax.broadcasted_iota(jnp.int32, (size, 2 * rank), 1) < rank

    def project(m):
        for k in range(slots - 1, -1, -1):
            both = jnp.concatenate([acts[k, m], delta[k]], axis=0)
            out = jnp.dot(both, dense[k], preferred_element_type=jnp.float32)
            parts[m * slots + k] = jnp.where(
                low(tokens), out[:tokens], out[tokens:]
            ).astype(jnp.bfloat16)
            owner, copy = part_copy(m, k)

            @pl.when(owner != me)
            def _():
                copy.start()

    def build():
        tiles_load.wait()
        r_in = lax.broadcasted_iota(jnp.int32, (2 * rank, 2 * rank), 0)
        r_out = lax.broadcasted_iota(jnp.int32, (2 * rank, 2 * rank), 1)
        moved = r_out - rank
        from_row = jnp.where(
            r_out < rank, r_out,
            rank + jnp.where(moved < half, 2 * moved, 2 * (moved - half) + 1),
        )
        shuffle = jnp.where(r_in == from_row, 1.0, 0.0).astype(jnp.bfloat16)
        for k in range(slots):
            for b in range(heads):
                wanted = tensor * heads + b
                pick = 0
                found = 0
                for j in range(n_tiles):
                    hit = blocks[k, 0, j] == wanted
                    pick = jnp.where(hit, j, pick)
                    found = jnp.where(hit, 1, found)
                block = jnp.dot(tiles[k, pick], shuffle, preferred_element_type=jnp.float32)
                dense[k, pl.ds(b * hs, hs), :] = jnp.where(found == 1, block, 0.0).astype(jnp.bfloat16)

    def z_copy(r, o):
        return pltpu.make_async_remote_copy(
            src_ref=zbuf.at[r, z], dst_ref=zbuf.at[r, z],
            send_sem=z_send.at[r, o - 1], recv_sem=z_recv.at[r, o - 1],
            device_id=at(lax.rem(z + o, n_z), me), device_id_type=MESH,
        )

    def x_copy(r, o):
        n = r * ring + me
        return pltpu.make_async_remote_copy(
            src_ref=sk.at[n], dst_ref=sk.at[n],
            send_sem=x_send.at[r, o - 1], recv_sem=x_recv.at[r, o - 1],
            device_id=at(z, lax.rem(me + o, ring)), device_id_type=MESH,
        )

    def outer(r):
        n = r * ring + me
        for s in range(ring - 1):
            pltpu.make_async_copy(red.at[r, s], red.at[r, s], part_recv.at[r, s]).wait()
        near = parts[n].astype(jnp.float32)
        for s in range(n_tensor - 1):
            near = near + red[r, s].astype(jnp.float32)
        far = red[r, n_tensor - 1].astype(jnp.float32)
        for s in range(n_tensor, ring - 1):
            far = far + red[r, s].astype(jnp.float32)
        x = jnp.concatenate([near, far], axis=0)
        y = jnp.where(low(2 * tokens), x, pltpu.roll(x, rank, 1))
        t = lax.dot_general(
            x, y, (((0,), (0,)), ((), ())), precision=lax.Precision.HIGHEST,
            preferred_element_type=jnp.float32,
        )
        out = jnp.where(low(half), t[rank : rank + half], t[rank + half :]) * scale
        zbuf[r, z] = jnp.where(lax.rem(n, slots) < live, out, 0.0).astype(jnp.bfloat16)
        for o in range(1, n_z):
            z_copy(r, o).start()

    def finish(r):
        for o in range(1, n_z):
            z_copy(r, o).wait_recv()
        total = zbuf[r, 0].astype(jnp.float32)
        for zz in range(1, n_z):
            total = total + zbuf[r, zz].astype(jnp.float32)
        sk[r * ring + me] = total.astype(jnp.bfloat16)
        for o in range(1, ring):
            x_copy(r, o).start()

    mix_load.wait()
    acts_load(0).wait()
    for h in range(heads):
        for k in range(slots):
            slopes(0, k, h)
    greeted = (n_z - 1) + (ring - 1)

    @pl.when(jnp.logical_and(pipe > 0, pipe < n_pipe - 1))
    def _():
        pl.semaphore_wait(barrier, greeted + 2)

    @pl.when(jnp.logical_or(pipe == 0, pipe == n_pipe - 1))
    def _():
        pl.semaphore_wait(barrier, greeted + 1)

    def step(m, c):
        chain(m)

        @pl.when(m == 0)
        def _():
            build()

        project(m)

        for r in range(rounds - 1):
            @pl.when(m == (ring * (r + 1) - 1) // slots + 2)
            def _():
                outer(r)

        for r in range(rounds - 2):
            @pl.when(m == (ring * (r + 1) - 1) // slots + 4)
            def _():
                finish(r)

        return c

    lax.fori_loop(0, micro, step, 0)
    outer(rounds - 1)
    finish(rounds - 2)
    finish(rounds - 1)

    for r in range(rounds):
        for o in range(1, ring):
            x_copy(r, o).wait_recv()
    for n in range(slots * micro):
        wide[pl.ds(n * half, half), :] = sk[n].astype(jnp.float32)
    for k in range(slots):
        for i in range(half):
            sk_out[0, k, :, pl.ds(i * 2 * rank, 2 * rank)] = wide[
                pl.ds(k * half + i, micro, stride=slots * half), :
            ]

    def drain(m, c):
        @pl.when(pipe > 0)
        def _():
            for q in range(GROUPS):
                relay(m, q).wait_send()

        for k in range(slots):
            owner, copy = part_copy(m, k)

            @pl.when(owner != me)
            def _():
                copy.wait_send()

        return c

    lax.fori_loop(0, micro, drain, 0)
    for r in range(rounds):
        for o in range(1, n_z):
            z_copy(r, o).wait_send()
        for o in range(1, ring):
            x_copy(r, o).wait_send()


def shards(n_dp, n_pipe, n_tensor, grad_out, activations, mixing, proj_tiles, proj_blocks, section_sizes):
    micro, tokens, width = grad_out.shape
    slots = activations.shape[1]
    heads, hs = mixing.shape[2:4]
    n_tiles = proj_tiles.shape[2]
    rank = proj_tiles.shape[4] // 2
    units = micro * slots
    ring = 2 * n_tensor
    rounds = units // ring
    n_z = n_dp // 2
    bf16, f32 = jnp.bfloat16, jnp.float32
    hbm = pl.BlockSpec(memory_space=pltpu.HBM)
    vmem = pl.BlockSpec(memory_space=pltpu.VMEM)
    smem = pl.BlockSpec(memory_space=pltpu.SMEM)
    dma = pltpu.SemaphoreType.DMA
    gout, sk = pl.pallas_call(
        functools.partial(kernel, n_dp, n_pipe, n_tensor, 1.0 / math.sqrt(tokens * n_dp)),
        out_shape=(
            pltpu.VMEM((micro, tokens, width), bf16),
            pltpu.VMEM((1, slots, micro, rank * rank), f32),
        ),
        in_specs=[smem, smem, hbm, hbm, hbm, hbm],
        out_specs=(vmem, vmem),
        scratch_shapes=[
            pltpu.VMEM((slots, micro, tokens, width), bf16),
            pltpu.VMEM((micro, tokens, width), bf16),
            pltpu.VMEM((slots, heads, hs, hs), bf16),
            pltpu.VMEM((slots, n_tiles, hs, 2 * rank), bf16),
            pltpu.VMEM((slots, width, 2 * rank), bf16),
            pltpu.VMEM((slots, tokens, width), f32),
            pltpu.VMEM((slots, tokens, width), bf16),
            pltpu.VMEM((units, tokens, 2 * rank), bf16),
            pltpu.VMEM((rounds, ring - 1, tokens, 2 * rank), bf16),
            pltpu.VMEM((rounds, n_z, rank // 2, 2 * rank), bf16),
            pltpu.VMEM((units, rank // 2, 2 * rank), bf16),
            pltpu.VMEM((units * rank // 2, 2 * rank), f32),
            dma((micro,)), dma((micro,)), dma((2,)),
            dma((micro, GROUPS)), dma((micro, GROUPS)),
            dma((units,)), dma((rounds, ring - 1)),
            dma((rounds, n_z - 1)), dma((rounds, n_z - 1)),
            dma((rounds, ring - 1)), dma((rounds, ring - 1)),
        ],
        compiler_params=pltpu.CompilerParams(
            collective_id=0, has_side_effects=True, vmem_limit_bytes=40 << 20
        ),
    )(*[
        pltpu.with_memory_space_constraint(x, pltpu.HBM)
        for x in (section_sizes, proj_blocks.transpose(1, 0, 2), grad_out, activations, mixing, proj_tiles)
    ])
    return pl.pallas_call(
        store,
        out_shape=(
            jax.ShapeDtypeStruct((1,) + gout.shape, bf16), jax.ShapeDtypeStruct(sk.shape, f32),
        ),
        in_specs=[vmem, vmem],
        out_specs=(hbm, hbm),
        scratch_shapes=[dma((2,))],
        compiler_params=pltpu.CompilerParams(vmem_limit_bytes=1 << 20),
    )(*[pltpu.with_memory_space_constraint(x, pltpu.VMEM) for x in (gout, sk)])


def solution(mesh):
    return jax.shard_map(
        functools.partial(shards, mesh.shape["dp"], mesh.shape["pipe"], mesh.shape["tensor"]),
        mesh=mesh,
        in_specs=(
            P(None, "dp", "tensor"),
            P("pipe", None, None, "dp", "tensor"),
            P("pipe", None, "tensor", None, None),
            P("pipe", None, None, None, None),
            P("pipe", None, None),
            P(),
        ),
        out_specs=(P("pipe", None, "dp", "tensor"), P("pipe", None, None, None)),
        check_vma=False,
    )
```

```python
import functools
import math

import jax
import jax.numpy as jnp
from jax import lax
from jax.experimental import pallas as pl
from jax.experimental.pallas import tpu as pltpu
from jax.sharding import PartitionSpec as P

MESH = pl.DeviceIdType.MESH
GROUPS = 2


def silu_slope(value):
    half = jnp.tanh(0.5 * value) * 0.5
    sig = 0.5 + half
    return sig * (1.0 + value * (0.5 - half))


def store(gout, sk, gout_hbm, sk_hbm, sem):
    copies = [
        pltpu.make_async_copy(gout, gout_hbm.at[0], sem.at[0]),
        pltpu.make_async_copy(sk, sk_hbm, sem.at[1]),
    ]
    for copy in copies:
        copy.start()
    for copy in copies:
        copy.wait()


def kernel(
    n_dp, n_pipe, n_tensor, scale,
    sizes_hbm, blocks_hbm, grad_hbm, acts_hbm, mix_hbm, tiles_hbm,
    gout, sk_out,
    sizes, blocks, acts, gin, mix, tiles, dense, slope, delta, gathered, parts, red, zbuf, sk, wide,
    acts_sem, grad_sem, weight_sem, near_z, near_x,
    relay_send, relay_recv, part_send, part_recv, z_send, z_recv, x_send, x_recv,
):
    slots, micro, tokens, width = acts.shape
    heads = mix.shape[1]
    hs = mix.shape[2]
    n_tiles = tiles.shape[1]
    rank = tiles.shape[3] // 2
    half = rank // 2
    ring = 2 * n_tensor
    n_z = n_dp // 2
    rounds = zbuf.shape[0]
    dp = lax.axis_index("dp")
    pipe = lax.axis_index("pipe")
    tensor = lax.axis_index("tensor")
    z = dp // 2
    side = lax.rem(dp, 2)
    me = side * n_tensor + tensor
    top = pipe == n_pipe - 1

    def at(zz, u, p=None):
        return {
            "dp": zz * 2 + u // n_tensor,
            "pipe": pipe if p is None else p,
            "tensor": lax.rem(u, n_tensor),
        }

    mix_load = pltpu.make_async_copy(mix_hbm.at[0], mix, weight_sem.at[0])
    tiles_load = pltpu.make_async_copy(tiles_hbm.at[0], tiles, weight_sem.at[1])

    def acts_load(m):
        return pltpu.make_async_copy(acts_hbm.at[0, :, m], acts.at[:, m], acts_sem.at[m])

    def grad_load(m):
        return pltpu.make_async_copy(grad_hbm.at[m], gin.at[m], grad_sem.at[m])

    sizes_load = pltpu.make_async_copy(sizes_hbm, sizes, weight_sem.at[2])
    blocks_load = pltpu.make_async_copy(blocks_hbm, blocks, weight_sem.at[3])
    mix_load.start()
    acts_load(0).start()

    @pl.when(top)
    def _():
        grad_load(0).start()

    barrier = pltpu.get_barrier_semaphore()

    def greet(where):
        pl.semaphore_signal(barrier, inc=1, device_id=where, device_id_type=MESH)

    @pl.when(pipe < n_pipe - 1)
    def _():
        greet(at(z, me, pipe + 1))

    @pl.when(pipe > 0)
    def _():
        greet(at(z, me, pipe - 1))

    beside_z = [at(lax.rem(z + o, n_z), me) for o in (1, n_z - 1)]
    beside_x = [at(z, lax.rem(me + o, ring)) for o in (1, ring - 1)]
    for where in beside_z + beside_x:
        greet(where)
    sizes_load.start()
    blocks_load.start()
    tiles_load.start()

    def tell(i):
        for where in beside_z:
            pl.semaphore_signal(near_z.at[i], inc=1, device_id=where, device_id_type=MESH)
        for where in beside_x:
            pl.semaphore_signal(near_x.at[i], inc=1, device_id=where, device_id_type=MESH)

    def hear(i):
        pl.semaphore_wait(near_z.at[i], 2)
        pl.semaphore_wait(near_x.at[i], 2)

    def load_rest(m, c):
        acts_load(m).start()

        @pl.when(top)
        def _():
            grad_load(m).start()

        return c

    lax.fori_loop(1, micro, load_rest, 0)

    def slopes(m, k, h):
        cols = pl.ds(h * hs, hs)
        pre = jnp.dot(acts[k, m, :, cols], mix[k, h], preferred_element_type=jnp.float32)
        slope[k, :, cols] = silu_slope(pre)

    def relay(m, q):
        cols = pl.ds(q * (width // GROUPS), width // GROUPS)
        return pltpu.make_async_remote_copy(
            src_ref=gout.at[m, :, cols], dst_ref=gin.at[m, :, cols],
            send_sem=relay_send.at[m, q], recv_sem=relay_recv.at[m, q],
            device_id=at(z, me, lax.rem(pipe + n_pipe - 1, n_pipe)), device_id_type=MESH,
        )

    def part_copy(m, k):
        n = m * slots + k
        owner = lax.rem(n, ring)
        turn = n // ring
        gap = lax.rem(tensor - lax.rem(owner, n_tensor) + n_tensor, n_tensor)
        slot = jnp.where(owner // n_tensor == side, gap - 1, n_tensor - 1 + gap)
        slot = jnp.maximum(slot, 0)
        return owner, pltpu.make_async_remote_copy(
            src_ref=parts.at[n], dst_ref=red.at[turn, slot],
            send_sem=part_send.at[n], recv_sem=part_recv.at[turn, slot],
            device_id=at(z, owner), device_id_type=MESH,
        )

    def low(size):
        return lax.broadcasted_iota(jnp.int32, (size, 2 * rank), 1) < rank

    def group(q):
        return range(q * heads // GROUPS, (q + 1) * heads // GROUPS)

    def project(m, q, k):
        cols = pl.ds(q * (width // GROUPS), width // GROUPS)
        both = jnp.concatenate([acts[k, m, :, cols], delta[k, :, cols]], axis=0)
        out = jnp.dot(both, dense[k, cols], preferred_element_type=jnp.float32)
        part = jnp.where(low(tokens), out[:tokens], out[tokens:])
        if q > 0:
            part = part + gathered[k]
        if q < GROUPS - 1:
            gathered[k] = part
        else:
            parts[m * slots + k] = part.astype(jnp.bfloat16)

    def send_parts(m):
        for k in range(slots - 1, -1, -1):
            owner, copy = part_copy(m, k)

            @pl.when(owner != me)
            def _():
                copy.start()

    def chain(m, q, after):
        some = group(q)
        g = {h: gin[m, :, pl.ds(h * hs, hs)] for h in some}
        for k in range(slots - 1, -1, -1):
            back = {}
            for h in some:
                cols = pl.ds(h * hs, hs)
                d = (g[h].astype(jnp.float32) * slope[k, :, cols]).astype(jnp.bfloat16)
                delta[k, :, cols] = d
                back[h] = lax.dot_general(
                    d, mix[k, h], (((1,), (1,)), ((), ())), preferred_element_type=jnp.float32
                )
            for h in some:
                slopes(after, k, h)
            if q > 0:
                project(m, q - 1, k)
            else:
                project(jnp.maximum(m - 1, 0), GROUPS - 1, k)
            for h in some:
                moved = (g[h].astype(jnp.float32) + back[h]).astype(jnp.bfloat16)
                g[h] = jnp.where(k < sizes[pipe], moved, g[h])
        for h in some:
            gout[m, :, pl.ds(h * hs, hs)] = g[h]

    def build(q):
        r_in = lax.broadcasted_iota(jnp.int32, (2 * rank, 2 * rank), 0)
        r_out = lax.broadcasted_iota(jnp.int32, (2 * rank, 2 * rank), 1)
        moved = r_out - rank
        from_row = jnp.where(
            r_out < rank, r_out,
            rank + jnp.where(moved < half, 2 * moved, 2 * (moved - half) + 1),
        )
        shuffle = jnp.where(r_in == from_row, 1.0, 0.0).astype(jnp.bfloat16)
        for k in range(slots):
            for b in group(q):
                wanted = tensor * heads + b
                pick = 0
                found = 0
                for j in range(n_tiles):
                    hit = blocks[k, 0, j] == wanted
                    pick = jnp.where(hit, j, pick)
                    found = jnp.where(hit, 1, found)
                block = jnp.dot(tiles[k, pick], shuffle, preferred_element_type=jnp.float32)
                dense[k, pl.ds(b * hs, hs), :] = jnp.where(found == 1, block, 0.0).astype(jnp.bfloat16)

    def z_copy(r, o):
        return pltpu.make_async_remote_copy(
            src_ref=zbuf.at[r, z], dst_ref=zbuf.at[r, z],
            send_sem=z_send.at[r, o - 1], recv_sem=z_recv.at[r, o - 1],
            device_id=at(lax.rem(z + o, n_z), me), device_id_type=MESH,
        )

    def x_copy(r, o):
        n = r * ring + me
        return pltpu.make_async_remote_copy(
            src_ref=sk.at[n], dst_ref=sk.at[n],
            send_sem=x_send.at[r, o - 1], recv_sem=x_recv.at[r, o - 1],
            device_id=at(z, lax.rem(me + o, ring)), device_id_type=MESH,
        )

    def outer(r):
        n = r * ring + me
        for s in range(ring - 1):
            pltpu.make_async_copy(red.at[r, s], red.at[r, s], part_recv.at[r, s]).wait()
        near = parts[n].astype(jnp.float32)
        for s in range(n_tensor - 1):
            near = near + red[r, s].astype(jnp.float32)
        far = red[r, n_tensor - 1].astype(jnp.float32)
        for s in range(n_tensor, ring - 1):
            far = far + red[r, s].astype(jnp.float32)
        x = jnp.concatenate([near, far], axis=0)
        y = jnp.where(low(2 * tokens), x, pltpu.roll(x, rank, 1))
        t = lax.dot_general(
            x, y, (((0,), (0,)), ((), ())), precision=lax.Precision.HIGHEST,
            preferred_element_type=jnp.float32,
        )
        out = jnp.where(low(half), t[rank : rank + half], t[rank + half :]) * scale
        zbuf[r, z] = jnp.where(lax.rem(n, slots) < sizes[pipe], out, 0.0).astype(jnp.bfloat16)
        for o in range(1, n_z):
            z_copy(r, o).start()

    def finish(r):
        for o in range(1, n_z):
            z_copy(r, o).wait_recv()
        total = zbuf[r, 0].astype(jnp.float32)
        for zz in range(1, n_z):
            total = total + zbuf[r, zz].astype(jnp.float32)
        sk[r * ring + me] = total.astype(jnp.bfloat16)
        for o in range(1, ring):
            x_copy(r, o).start()

    mix_load.wait()
    acts_load(0).wait()

    def start_slopes(q):
        for h in group(q):
            for k in range(slots):
                slopes(0, k, h)

    start_slopes(0)
    sizes_load.wait()

    @pl.when(jnp.logical_and(pipe > 0, pipe < n_pipe - 1))
    def _():
        pl.semaphore_wait(barrier, 6)

    @pl.when(jnp.logical_or(pipe == 0, pipe == n_pipe - 1))
    def _():
        pl.semaphore_wait(barrier, 5)

    tell(0)

    @pl.when(jnp.logical_not(top))
    def _():
        tiles_load.wait()
        blocks_load.wait()
        for q in range(GROUPS):
            build(q)
        hear(0)
        tell(1)
        for q in range(1, GROUPS):
            start_slopes(q)
        hear(1)
        tell(2)

    def step(m, c):
        after = jnp.minimum(m + 1, micro - 1)

        @pl.when(top)
        def _():
            grad_load(m).wait()

        @pl.when(m + 1 < micro)
        def _():
            acts_load(after).wait()

        for q in range(GROUPS):
            @pl.when(jnp.logical_not(top))
            def _():
                relay(m, q).wait_recv()

            chain(m, q, after)

            @pl.when(pipe > 0)
            def _():
                relay(m, q).start()

            if q == 0:
                @pl.when(m == 1)
                def _():
                    hear(2)

                @pl.when(m > 0)
                def _():
                    send_parts(m - 1)

            @pl.when(jnp.logical_and(m == 0, top))
            def _():
                if q == 0:
                    tiles_load.wait()
                    blocks_load.wait()
                build(q)
                if q + 1 < GROUPS:
                    start_slopes(q + 1)
                if q == 0:
                    hear(0)
                    tell(1)
                if q == GROUPS - 1:
                    hear(1)
                    tell(2)

        for r in range(rounds - 1):
            @pl.when(m == (ring * (r + 1) - 1) // slots + 2)
            def _():
                outer(r)

        for r in range(rounds - 2):
            @pl.when(m == (ring * (r + 1) - 1) // slots + 4)
            def _():
                finish(r)

        return c

    lax.fori_loop(0, micro, step, 0)
    for k in range(slots - 1, -1, -1):
        project(micro - 1, GROUPS - 1, k)
    send_parts(micro - 1)
    outer(rounds - 1)
    finish(rounds - 2)

    def drain(m, c):
        @pl.when(pipe > 0)
        def _():
            for q in range(GROUPS):
                relay(m, q).wait_send()

        for k in range(slots):
            owner, copy = part_copy(m, k)

            @pl.when(owner != me)
            def _():
                copy.wait_send()

        return c

    lax.fori_loop(0, micro, drain, 0)
    for r in range(rounds):
        for o in range(1, n_z):
            z_copy(r, o).wait_send()
    finish(rounds - 1)

    def widen(r):
        for o in range(1, ring):
            x_copy(r, o).wait_recv()
        for n in range(r * ring, (r + 1) * ring):
            wide[pl.ds(n * half, half), :] = sk[n].astype(jnp.float32)

    for r in range(rounds):
        widen(r)
    for k in range(slots):
        for i in range(half):
            sk_out[0, k, :, pl.ds(i * 2 * rank, 2 * rank)] = wide[
                pl.ds(k * half + i, micro, stride=slots * half), :
            ]
    for r in range(rounds):
        for o in range(1, ring):
            x_copy(r, o).wait_send()


def shards(n_dp, n_pipe, n_tensor, grad_out, activations, mixing, proj_tiles, proj_blocks, section_sizes):
    micro, tokens, width = grad_out.shape
    slots = activations.shape[1]
    heads, hs = mixing.shape[2:4]
    n_tiles = proj_tiles.shape[2]
    rank = proj_tiles.shape[4] // 2
    units = micro * slots
    ring = 2 * n_tensor
    rounds = units // ring
    n_z = n_dp // 2
    bf16, f32 = jnp.bfloat16, jnp.float32
    hbm = pl.BlockSpec(memory_space=pltpu.HBM)
    vmem = pl.BlockSpec(memory_space=pltpu.VMEM)
    dma = pltpu.SemaphoreType.DMA
    gout, sk = pl.pallas_call(
        functools.partial(kernel, n_dp, n_pipe, n_tensor, 1.0 / math.sqrt(tokens * n_dp)),
        out_shape=(
            pltpu.VMEM((micro, tokens, width), bf16),
            pltpu.VMEM((1, slots, micro, rank * rank), f32),
        ),
        in_specs=[hbm] * 6,
        out_specs=(vmem, vmem),
        scratch_shapes=[
            pltpu.SMEM(section_sizes.shape, jnp.int32),
            pltpu.SMEM((slots, 1, n_tiles), jnp.int32),
            pltpu.VMEM((slots, micro, tokens, width), bf16),
            pltpu.VMEM((micro, tokens, width), bf16),
            pltpu.VMEM((slots, heads, hs, hs), bf16),
            pltpu.VMEM((slots, n_tiles, hs, 2 * rank), bf16),
            pltpu.VMEM((slots, width, 2 * rank), bf16),
            pltpu.VMEM((slots, tokens, width), f32),
            pltpu.VMEM((slots, tokens, width), bf16),
            pltpu.VMEM((slots, tokens, 2 * rank), f32),
            pltpu.VMEM((units, tokens, 2 * rank), bf16),
            pltpu.VMEM((rounds, ring - 1, tokens, 2 * rank), bf16),
            pltpu.VMEM((rounds, n_z, rank // 2, 2 * rank), bf16),
            pltpu.VMEM((units, rank // 2, 2 * rank), bf16),
            pltpu.VMEM((units * rank // 2, 2 * rank), f32),
            dma((micro,)), dma((micro,)), dma((4,)),
            pltpu.SemaphoreType.REGULAR((3,)), pltpu.SemaphoreType.REGULAR((3,)),
            dma((micro, GROUPS)), dma((micro, GROUPS)),
            dma((units,)), dma((rounds, ring - 1)),
            dma((rounds, n_z - 1)), dma((rounds, n_z - 1)),
            dma((rounds, ring - 1)), dma((rounds, ring - 1)),
        ],
        compiler_params=pltpu.CompilerParams(
            collective_id=0, has_side_effects=True, vmem_limit_bytes=40 << 20
        ),
    )(*[
        pltpu.with_memory_space_constraint(x, pltpu.HBM)
        for x in (section_sizes, proj_blocks.transpose(1, 0, 2), grad_out, activations, mixing, proj_tiles)
    ])
    return pl.pallas_call(
        store,
        out_shape=(
            jax.ShapeDtypeStruct((1,) + gout.shape, bf16), jax.ShapeDtypeStruct(sk.shape, f32),
        ),
        in_specs=[vmem, vmem],
        out_specs=(hbm, hbm),
        scratch_shapes=[dma((2,))],
        compiler_params=pltpu.CompilerParams(vmem_limit_bytes=1 << 20),
    )(*[pltpu.with_memory_space_constraint(x, pltpu.VMEM) for x in (gout, sk)])


def solution(mesh):
    return jax.shard_map(
        functools.partial(shards, mesh.shape["dp"], mesh.shape["pipe"], mesh.shape["tensor"]),
        mesh=mesh,
        in_specs=(
            P(None, "dp", "tensor"),
            P("pipe", None, None, "dp", "tensor"),
            P("pipe", None, "tensor", None, None),
            P("pipe", None, None, None, None),
            P("pipe", None, None),
            P(),
        ),
        out_specs=(P("pipe", None, "dp", "tensor"), P("pipe", None, None, None)),
        check_vma=False,
    )
```

```python
import functools
import math

import jax
import jax.numpy as jnp
from jax import lax
from jax.experimental import pallas as pl
from jax.experimental.pallas import tpu as pltpu
from jax.sharding import PartitionSpec as P

MESH = pl.DeviceIdType.MESH
GROUPS = 2


def silu_slope(value):
    half = jnp.tanh(0.5 * value) * 0.5
    sig = 0.5 + half
    return sig * (1.0 + value * (0.5 - half))


def store(gout, sk, gout_hbm, sk_hbm, sem):
    copies = [
        pltpu.make_async_copy(gout, gout_hbm.at[0], sem.at[0]),
        pltpu.make_async_copy(sk, sk_hbm, sem.at[1]),
    ]
    for copy in copies:
        copy.start()
    for copy in copies:
        copy.wait()


def kernel(
    n_dp, n_pipe, n_tensor, scale,
    sizes_hbm, blocks_hbm, grad_hbm, acts_hbm, mix_hbm, tiles_hbm,
    gout, sk_out,
    sizes, blocks, acts, gin, mix, tiles, dense, slope, delta, gathered, parts, red, zbuf, sk, square,
    acts_sem, grad_sem, weight_sem, near_z, near_x,
    relay_send, relay_recv, part_send, part_recv, z_send, z_recv, x_send, x_recv,
):
    slots, micro, tokens, width = acts.shape
    heads = mix.shape[1]
    hs = mix.shape[2]
    n_tiles = tiles.shape[1]
    rank = tiles.shape[3] // 2
    half = rank // 2
    ring = 2 * n_tensor
    n_z = n_dp // 2
    rounds = zbuf.shape[0]
    dp = lax.axis_index("dp")
    pipe = lax.axis_index("pipe")
    tensor = lax.axis_index("tensor")
    z = dp // 2
    side = lax.rem(dp, 2)
    me = side * n_tensor + tensor
    top = pipe == n_pipe - 1

    def at(zz, u, p=None):
        return {
            "dp": zz * 2 + u // n_tensor,
            "pipe": pipe if p is None else p,
            "tensor": lax.rem(u, n_tensor),
        }

    mix_load = pltpu.make_async_copy(mix_hbm.at[0], mix, weight_sem.at[0])
    tiles_load = pltpu.make_async_copy(tiles_hbm.at[0], tiles, weight_sem.at[1])

    def acts_load(m):
        return pltpu.make_async_copy(acts_hbm.at[0, :, m], acts.at[:, m], acts_sem.at[m])

    def grad_load(m):
        return pltpu.make_async_copy(grad_hbm.at[m], gin.at[m], grad_sem.at[m])

    sizes_load = pltpu.make_async_copy(sizes_hbm, sizes, weight_sem.at[2])
    blocks_load = pltpu.make_async_copy(blocks_hbm, blocks, weight_sem.at[3])
    mix_load.start()
    acts_load(0).start()

    @pl.when(top)
    def _():
        grad_load(0).start()

    barrier = pltpu.get_barrier_semaphore()

    def greet(where):
        pl.semaphore_signal(barrier, inc=1, device_id=where, device_id_type=MESH)

    @pl.when(pipe < n_pipe - 1)
    def _():
        greet(at(z, me, pipe + 1))

    @pl.when(pipe > 0)
    def _():
        greet(at(z, me, pipe - 1))

    beside_z = [at(lax.rem(z + o, n_z), me) for o in (1, n_z - 1)]
    beside_x = [at(z, lax.rem(me + o, ring)) for o in (1, ring - 1)]
    for where in beside_z + beside_x:
        greet(where)
    sizes_load.start()
    blocks_load.start()
    tiles_load.start()

    def tell(i):
        for where in beside_z:
            pl.semaphore_signal(near_z.at[i], inc=1, device_id=where, device_id_type=MESH)
        for where in beside_x:
            pl.semaphore_signal(near_x.at[i], inc=1, device_id=where, device_id_type=MESH)

    def hear(i):
        pl.semaphore_wait(near_z.at[i], 2)
        pl.semaphore_wait(near_x.at[i], 2)

    def load_rest(m, c):
        acts_load(m).start()

        @pl.when(top)
        def _():
            grad_load(m).start()

        return c

    lax.fori_loop(1, micro, load_rest, 0)

    def slopes(m, k, h):
        cols = pl.ds(h * hs, hs)
        pre = jnp.dot(acts[k, m, :, cols], mix[k, h], preferred_element_type=jnp.float32)
        slope[k, :, cols] = silu_slope(pre)

    def relay(m, q):
        cols = pl.ds(q * (width // GROUPS), width // GROUPS)
        return pltpu.make_async_remote_copy(
            src_ref=gout.at[m, :, cols], dst_ref=gin.at[m, :, cols],
            send_sem=relay_send.at[m, q], recv_sem=relay_recv.at[m, q],
            device_id=at(z, me, lax.rem(pipe + n_pipe - 1, n_pipe)), device_id_type=MESH,
        )

    def part_copy(m, k):
        n = m * slots + k
        owner = lax.rem(n, ring)
        turn = n // ring
        gap = lax.rem(tensor - lax.rem(owner, n_tensor) + n_tensor, n_tensor)
        slot = jnp.where(owner // n_tensor == side, gap - 1, n_tensor - 1 + gap)
        slot = jnp.maximum(slot, 0)
        return owner, pltpu.make_async_remote_copy(
            src_ref=parts.at[n], dst_ref=red.at[turn, slot],
            send_sem=part_send.at[n], recv_sem=part_recv.at[turn, slot],
            device_id=at(z, owner), device_id_type=MESH,
        )

    def low(size):
        return lax.broadcasted_iota(jnp.int32, (size, 2 * rank), 1) < rank

    def group(q):
        return range(q * heads // GROUPS, (q + 1) * heads // GROUPS)

    def project(m, q, k):
        cols = pl.ds(q * (width // GROUPS), width // GROUPS)
        both = jnp.concatenate([acts[k, m, :, cols], delta[k, :, cols]], axis=0)
        out = jnp.dot(both, dense[k, cols], preferred_element_type=jnp.float32)
        part = jnp.where(low(tokens), out[:tokens], out[tokens:])
        if q > 0:
            part = part + gathered[k]
        if q < GROUPS - 1:
            gathered[k] = part
        else:
            parts[m * slots + k] = part.astype(jnp.bfloat16)

    def send_parts(m):
        for k in range(slots - 1, -1, -1):
            owner, copy = part_copy(m, k)

            @pl.when(owner != me)
            def _():
                copy.start()

    def chain(m, q, after):
        some = group(q)
        g = {h: gin[m, :, pl.ds(h * hs, hs)] for h in some}
        for k in range(slots - 1, -1, -1):
            back = {}
            for h in some:
                cols = pl.ds(h * hs, hs)
                d = (g[h].astype(jnp.float32) * slope[k, :, cols]).astype(jnp.bfloat16)
                delta[k, :, cols] = d
                back[h] = lax.dot_general(
                    d, mix[k, h], (((1,), (1,)), ((), ())), preferred_element_type=jnp.float32
                )
            for h in some:
                slopes(after, k, h)
            if q > 0:
                project(m, q - 1, k)
            else:
                project(jnp.maximum(m - 1, 0), GROUPS - 1, k)
            for h in some:
                moved = (g[h].astype(jnp.float32) + back[h]).astype(jnp.bfloat16)
                g[h] = jnp.where(k < sizes[pipe], moved, g[h])
        for h in some:
            gout[m, :, pl.ds(h * hs, hs)] = g[h]

    def build(q):
        for k in range(slots):
            for b in group(q):
                wanted = tensor * heads + b
                pick = 0
                found = 0
                for j in range(n_tiles):
                    hit = blocks[k, 0, j] == wanted
                    pick = jnp.where(hit, j, pick)
                    found = jnp.where(hit, 1, found)
                block = tiles[k, pick]
                dense[k, pl.ds(b * hs, hs), :] = jnp.where(found == 1, block, jnp.zeros_like(block))

    def z_copy(r, o):
        return pltpu.make_async_remote_copy(
            src_ref=zbuf.at[r, z], dst_ref=zbuf.at[r, z],
            send_sem=z_send.at[r, o - 1], recv_sem=z_recv.at[r, o - 1],
            device_id=at(lax.rem(z + o, n_z), me), device_id_type=MESH,
        )

    def x_copy(r, o):
        n = r * ring + me
        return pltpu.make_async_remote_copy(
            src_ref=sk.at[n], dst_ref=sk.at[n],
            send_sem=x_send.at[r, o - 1], recv_sem=x_recv.at[r, o - 1],
            device_id=at(z, lax.rem(me + o, ring)), device_id_type=MESH,
        )

    def outer(r):
        n = r * ring + me
        for s in range(ring - 1):
            pltpu.make_async_copy(red.at[r, s], red.at[r, s], part_recv.at[r, s]).wait()
        near = parts[n].astype(jnp.float32)
        for s in range(n_tensor - 1):
            near = near + red[r, s].astype(jnp.float32)
        far = red[r, n_tensor - 1].astype(jnp.float32)
        for s in range(n_tensor, ring - 1):
            far = far + red[r, s].astype(jnp.float32)
        x = jnp.concatenate([near, far], axis=0)
        y = jnp.where(low(2 * tokens), x, pltpu.roll(x, rank, 1))
        t = lax.dot_general(
            x, y, (((0,), (0,)), ((), ())), precision=lax.Precision.HIGHEST,
            preferred_element_type=jnp.float32,
        )
        square[...] = t[rank:]
        out = jnp.where(
            low(half), square[pl.ds(0, half, stride=2), :], square[pl.ds(1, half, stride=2), :]
        ) * scale
        zbuf[r, z] = jnp.where(lax.rem(n, slots) < sizes[pipe], out, 0.0).astype(jnp.bfloat16)
        for o in range(1, n_z):
            z_copy(r, o).start()

    def finish(r):
        for o in range(1, n_z):
            z_copy(r, o).wait_recv()
        total = zbuf[r, 0].astype(jnp.float32)
        for zz in range(1, n_z):
            total = total + zbuf[r, zz].astype(jnp.float32)
        sk[r * ring + me] = total.astype(jnp.bfloat16)
        for o in range(1, ring):
            x_copy(r, o).start()

    mix_load.wait()
    acts_load(0).wait()

    def start_slopes(q):
        for h in group(q):
            for k in range(slots):
                slopes(0, k, h)

    start_slopes(0)
    sizes_load.wait()

    @pl.when(jnp.logical_and(pipe > 0, pipe < n_pipe - 1))
    def _():
        pl.semaphore_wait(barrier, 6)

    @pl.when(jnp.logical_or(pipe == 0, pipe == n_pipe - 1))
    def _():
        pl.semaphore_wait(barrier, 5)

    tell(0)

    @pl.when(jnp.logical_not(top))
    def _():
        tiles_load.wait()
        blocks_load.wait()
        for q in range(GROUPS):
            build(q)
        hear(0)
        tell(1)
        for q in range(1, GROUPS):
            start_slopes(q)
        hear(1)
        tell(2)

    def step(m, c):
        after = jnp.minimum(m + 1, micro - 1)

        @pl.when(top)
        def _():
            grad_load(m).wait()

        @pl.when(m + 1 < micro)
        def _():
            acts_load(after).wait()

        for q in range(GROUPS):
            @pl.when(jnp.logical_not(top))
            def _():
                relay(m, q).wait_recv()

            chain(m, q, after)

            @pl.when(pipe > 0)
            def _():
                relay(m, q).start()

            if q == 0:
                @pl.when(m == 1)
                def _():
                    hear(2)

                @pl.when(m > 0)
                def _():
                    send_parts(m - 1)

            @pl.when(jnp.logical_and(m == 0, top))
            def _():
                if q == 0:
                    tiles_load.wait()
                    blocks_load.wait()
                build(q)
                if q + 1 < GROUPS:
                    start_slopes(q + 1)
                if q == 0:
                    hear(0)
                    tell(1)
                if q == GROUPS - 1:
                    hear(1)
                    tell(2)

        for r in range(rounds - 1):
            @pl.when(m == (ring * (r + 1) - 1) // slots + 2)
            def _():
                outer(r)

        for r in range(rounds - 2):
            @pl.when(m == (ring * (r + 1) - 1) // slots + 4)
            def _():
                finish(r)

        return c

    lax.fori_loop(0, micro, step, 0)
    for k in range(slots - 1, -1, -1):
        project(micro - 1, GROUPS - 1, k)
    send_parts(micro - 1)
    outer(rounds - 1)

    def drain(m, c):
        @pl.when(pipe > 0)
        def _():
            for q in range(GROUPS):
                relay(m, q).wait_send()

        for k in range(slots):
            owner, copy = part_copy(m, k)

            @pl.when(owner != me)
            def _():
                copy.wait_send()

        return c

    lax.fori_loop(0, micro, drain, 0)
    def unpack(r):
        for o in range(1, ring):
            x_copy(r, o).wait_recv()
        for n in range(r * ring, (r + 1) * ring):
            m, k = divmod(n, slots)
            rows = pl.ds(k * half * micro + m, half, stride=micro)
            sk_out[rows, :] = sk[n].astype(jnp.float32)

    finish(rounds - 2)
    for r in range(rounds - 2):
        unpack(r)
    for r in range(rounds):
        for o in range(1, n_z):
            z_copy(r, o).wait_send()
    finish(rounds - 1)
    for r in range(rounds - 2, rounds):
        unpack(r)
    for r in range(rounds):
        for o in range(1, ring):
            x_copy(r, o).wait_send()


def shards(n_dp, n_pipe, n_tensor, grad_out, activations, mixing, proj_tiles, proj_blocks, section_sizes):
    micro, tokens, width = grad_out.shape
    slots = activations.shape[1]
    heads, hs = mixing.shape[2:4]
    n_tiles = proj_tiles.shape[2]
    rank = proj_tiles.shape[4] // 2
    units = micro * slots
    ring = 2 * n_tensor
    rounds = units // ring
    n_z = n_dp // 2
    bf16, f32 = jnp.bfloat16, jnp.float32
    hbm = pl.BlockSpec(memory_space=pltpu.HBM)
    vmem = pl.BlockSpec(memory_space=pltpu.VMEM)
    dma = pltpu.SemaphoreType.DMA
    gout, sk = pl.pallas_call(
        functools.partial(kernel, n_dp, n_pipe, n_tensor, 1.0 / math.sqrt(tokens * n_dp)),
        out_shape=(
            pltpu.VMEM((micro, tokens, width), bf16),
            pltpu.VMEM((units * rank // 2, 2 * rank), f32),
        ),
        in_specs=[hbm] * 6,
        out_specs=(vmem, vmem),
        scratch_shapes=[
            pltpu.SMEM(section_sizes.shape, jnp.int32),
            pltpu.SMEM((slots, 1, n_tiles), jnp.int32),
            pltpu.VMEM((slots, micro, tokens, width), bf16),
            pltpu.VMEM((micro, tokens, width), bf16),
            pltpu.VMEM((slots, heads, hs, hs), bf16),
            pltpu.VMEM((slots, n_tiles, hs, 2 * rank), bf16),
            pltpu.VMEM((slots, width, 2 * rank), bf16),
            pltpu.VMEM((slots, tokens, width), f32),
            pltpu.VMEM((slots, tokens, width), bf16),
            pltpu.VMEM((slots, tokens, 2 * rank), f32),
            pltpu.VMEM((units, tokens, 2 * rank), bf16),
            pltpu.VMEM((rounds, ring - 1, tokens, 2 * rank), bf16),
            pltpu.VMEM((rounds, n_z, rank // 2, 2 * rank), bf16),
            pltpu.VMEM((units, rank // 2, 2 * rank), bf16),
            pltpu.VMEM((rank, 2 * rank), f32),
            dma((micro,)), dma((micro,)), dma((4,)),
            pltpu.SemaphoreType.REGULAR((3,)), pltpu.SemaphoreType.REGULAR((3,)),
            dma((micro, GROUPS)), dma((micro, GROUPS)),
            dma((units,)), dma((rounds, ring - 1)),
            dma((rounds, n_z - 1)), dma((rounds, n_z - 1)),
            dma((rounds, ring - 1)), dma((rounds, ring - 1)),
        ],
        compiler_params=pltpu.CompilerParams(
            collective_id=0, has_side_effects=True, vmem_limit_bytes=40 << 20
        ),
    )(*[
        pltpu.with_memory_space_constraint(x, pltpu.HBM)
        for x in (section_sizes, proj_blocks.transpose(1, 0, 2), grad_out, activations, mixing, proj_tiles)
    ])
    grads, sk = pl.pallas_call(
        store,
        out_shape=(
            jax.ShapeDtypeStruct((1,) + gout.shape, bf16), jax.ShapeDtypeStruct(sk.shape, f32),
        ),
        in_specs=[vmem, vmem],
        out_specs=(hbm, hbm),
        scratch_shapes=[dma((2,))],
        compiler_params=pltpu.CompilerParams(vmem_limit_bytes=1 << 20),
    )(*[pltpu.with_memory_space_constraint(x, pltpu.VMEM) for x in (gout, sk)])
    sk = sk.reshape(slots, rank // 2, micro, 2 * rank).transpose(0, 2, 1, 3)
    return grads, sk.reshape(1, slots, micro, rank * rank)


def solution(mesh):
    return jax.shard_map(
        functools.partial(shards, mesh.shape["dp"], mesh.shape["pipe"], mesh.shape["tensor"]),
        mesh=mesh,
        in_specs=(
            P(None, "dp", "tensor"),
            P("pipe", None, None, "dp", "tensor"),
            P("pipe", None, "tensor", None, None),
            P("pipe", None, None, None, None),
            P("pipe", None, None),
            P(),
        ),
        out_specs=(P("pipe", None, "dp", "tensor"), P("pipe", None, None, None)),
        check_vma=False,
    )
```

```python
import functools
import math

import jax
import jax.numpy as jnp
from jax import lax
from jax.experimental import pallas as pl
from jax.experimental.pallas import tpu as pltpu
from jax.sharding import PartitionSpec as P

MESH = pl.DeviceIdType.MESH
GROUPS = 2


def silu_slope(value):
    half = jnp.tanh(0.5 * value) * 0.5
    sig = 0.5 + half
    return sig * (1.0 + value * (0.5 - half))


def far_first(size):
    return sorted(range(1, size), key=lambda o: -min(o, size - o))


def store(gout, sk, gout_hbm, sk_hbm, sem):
    copies = [
        pltpu.make_async_copy(gout, gout_hbm.at[0], sem.at[0]),
        pltpu.make_async_copy(sk, sk_hbm, sem.at[1]),
    ]
    for copy in copies:
        copy.start()
    for copy in copies:
        copy.wait()


def kernel(
    n_dp, n_pipe, n_tensor, scale,
    sizes_hbm, blocks_hbm, grad_hbm, acts_hbm, mix_hbm, tiles_hbm,
    gout, sk_out,
    sizes, blocks, acts, gin, mix, tiles, dense, slope, delta, gathered, parts, red, zbuf, sk, square,
    acts_sem, grad_sem, weight_sem, near_z, near_x,
    relay_send, relay_recv, part_send, part_recv, z_send, z_recv, x_send, x_recv,
):
    slots, micro, tokens, width = acts.shape
    heads = mix.shape[1]
    hs = mix.shape[2]
    n_tiles = tiles.shape[1]
    rank = tiles.shape[3] // 2
    half = rank // 2
    ring = 2 * n_tensor
    n_z = n_dp // 2
    rounds = zbuf.shape[0]
    dp = lax.axis_index("dp")
    pipe = lax.axis_index("pipe")
    tensor = lax.axis_index("tensor")
    z = dp // 2
    side = lax.rem(dp, 2)
    me = side * n_tensor + tensor
    top = pipe == n_pipe - 1

    def at(zz, u, p=None):
        return {
            "dp": zz * 2 + u // n_tensor,
            "pipe": pipe if p is None else p,
            "tensor": lax.rem(u, n_tensor),
        }

    mix_load = pltpu.make_async_copy(mix_hbm.at[0], mix, weight_sem.at[0])
    tiles_load = pltpu.make_async_copy(tiles_hbm.at[0], tiles, weight_sem.at[1])

    def acts_load(m):
        return pltpu.make_async_copy(acts_hbm.at[0, :, m], acts.at[:, m], acts_sem.at[m])

    def grad_load(m):
        return pltpu.make_async_copy(grad_hbm.at[m], gin.at[m], grad_sem.at[m])

    sizes_load = pltpu.make_async_copy(sizes_hbm, sizes, weight_sem.at[2])
    blocks_load = pltpu.make_async_copy(blocks_hbm, blocks, weight_sem.at[3])
    mix_load.start()
    acts_load(0).start()

    @pl.when(top)
    def _():
        grad_load(0).start()

    barrier = pltpu.get_barrier_semaphore()

    def greet(where):
        pl.semaphore_signal(barrier, inc=1, device_id=where, device_id_type=MESH)

    @pl.when(pipe < n_pipe - 1)
    def _():
        greet(at(z, me, pipe + 1))

    @pl.when(pipe > 0)
    def _():
        greet(at(z, me, pipe - 1))

    beside_z = [at(lax.rem(z + o, n_z), me) for o in (1, n_z - 1)]
    beside_x = [at(z, lax.rem(me + o, ring)) for o in (1, ring - 1)]
    for where in beside_z + beside_x:
        greet(where)
    sizes_load.start()
    blocks_load.start()
    tiles_load.start()

    def tell(i):
        for where in beside_z:
            pl.semaphore_signal(near_z.at[i], inc=1, device_id=where, device_id_type=MESH)
        for where in beside_x:
            pl.semaphore_signal(near_x.at[i], inc=1, device_id=where, device_id_type=MESH)

    def hear(i):
        pl.semaphore_wait(near_z.at[i], 2)
        pl.semaphore_wait(near_x.at[i], 2)

    def load_rest(m, c):
        acts_load(m).start()

        @pl.when(top)
        def _():
            grad_load(m).start()

        return c

    lax.fori_loop(1, micro, load_rest, 0)

    def slopes(m, k, h):
        cols = pl.ds(h * hs, hs)
        pre = jnp.dot(acts[k, m, :, cols], mix[k, h], preferred_element_type=jnp.float32)
        slope[k, :, cols] = silu_slope(pre)

    def relay(m, q):
        cols = pl.ds(q * (width // GROUPS), width // GROUPS)
        return pltpu.make_async_remote_copy(
            src_ref=gout.at[m, :, cols], dst_ref=gin.at[m, :, cols],
            send_sem=relay_send.at[m, q], recv_sem=relay_recv.at[m, q],
            device_id=at(z, me, lax.rem(pipe + n_pipe - 1, n_pipe)), device_id_type=MESH,
        )

    def part_copy(m, k):
        n = m * slots + k
        owner = lax.rem(n, ring)
        turn = n // ring
        gap = lax.rem(tensor - lax.rem(owner, n_tensor) + n_tensor, n_tensor)
        slot = jnp.where(owner // n_tensor == side, gap - 1, n_tensor - 1 + gap)
        slot = jnp.maximum(slot, 0)
        return owner, pltpu.make_async_remote_copy(
            src_ref=parts.at[n], dst_ref=red.at[turn, slot],
            send_sem=part_send.at[n], recv_sem=part_recv.at[turn, slot],
            device_id=at(z, owner), device_id_type=MESH,
        )

    def low(size):
        return lax.broadcasted_iota(jnp.int32, (size, 2 * rank), 1) < rank

    def group(q):
        return range(q * heads // GROUPS, (q + 1) * heads // GROUPS)

    def project(m, q, k):
        cols = pl.ds(q * (width // GROUPS), width // GROUPS)
        both = jnp.concatenate([acts[k, m, :, cols], delta[k, :, cols]], axis=0)
        out = jnp.dot(both, dense[k, cols], preferred_element_type=jnp.float32)
        part = jnp.where(low(tokens), out[:tokens], out[tokens:])
        if q > 0:
            part = part + gathered[k]
        if q < GROUPS - 1:
            gathered[k] = part
        else:
            parts[m * slots + k] = part.astype(jnp.bfloat16)

    def send_parts(m):
        for k in range(slots - 1, -1, -1):
            owner, copy = part_copy(m, k)

            @pl.when(owner != me)
            def _():
                copy.start()

    def chain(m, q, after):
        some = group(q)
        g = {h: gin[m, :, pl.ds(h * hs, hs)] for h in some}
        for k in range(slots - 1, -1, -1):
            back = {}
            for h in some:
                cols = pl.ds(h * hs, hs)
                d = (g[h].astype(jnp.float32) * slope[k, :, cols]).astype(jnp.bfloat16)
                delta[k, :, cols] = d
                back[h] = lax.dot_general(
                    d, mix[k, h], (((1,), (1,)), ((), ())), preferred_element_type=jnp.float32
                )
            for h in some:
                slopes(after, k, h)
            if q > 0:
                project(m, q - 1, k)
            else:
                project(jnp.maximum(m - 1, 0), GROUPS - 1, k)
            for h in some:
                moved = (g[h].astype(jnp.float32) + back[h]).astype(jnp.bfloat16)
                g[h] = jnp.where(k < sizes[pipe], moved, g[h])
        for h in some:
            gout[m, :, pl.ds(h * hs, hs)] = g[h]

    def build(q):
        for k in range(slots):
            for b in group(q):
                wanted = tensor * heads + b
                pick = 0
                found = 0
                for j in range(n_tiles):
                    hit = blocks[k, 0, j] == wanted
                    pick = jnp.where(hit, j, pick)
                    found = jnp.where(hit, 1, found)
                block = tiles[k, pick]
                dense[k, pl.ds(b * hs, hs), :] = jnp.where(found == 1, block, jnp.zeros_like(block))

    def z_copy(r, o):
        return pltpu.make_async_remote_copy(
            src_ref=zbuf.at[r, z], dst_ref=zbuf.at[r, z],
            send_sem=z_send.at[r, o - 1], recv_sem=z_recv.at[r, o - 1],
            device_id=at(lax.rem(z + o, n_z), me), device_id_type=MESH,
        )

    def x_copy(r, o):
        n = r * ring + me
        return pltpu.make_async_remote_copy(
            src_ref=sk.at[n], dst_ref=sk.at[n],
            send_sem=x_send.at[r, o - 1], recv_sem=x_recv.at[r, o - 1],
            device_id=at(z, lax.rem(me + o, ring)), device_id_type=MESH,
        )

    def outer(r):
        n = r * ring + me
        for s in range(ring - 1):
            pltpu.make_async_copy(red.at[r, s], red.at[r, s], part_recv.at[r, s]).wait()
        near = parts[n].astype(jnp.float32)
        for s in range(n_tensor - 1):
            near = near + red[r, s].astype(jnp.float32)
        far = red[r, n_tensor - 1].astype(jnp.float32)
        for s in range(n_tensor, ring - 1):
            far = far + red[r, s].astype(jnp.float32)
        x = jnp.concatenate([near, far], axis=0)
        y = jnp.where(low(2 * tokens), x, pltpu.roll(x, rank, 1))
        t = lax.dot_general(
            x, y, (((0,), (0,)), ((), ())), precision=lax.Precision.HIGHEST,
            preferred_element_type=jnp.float32,
        )
        square[...] = t[rank:]
        out = jnp.where(
            low(half), square[pl.ds(0, half, stride=2), :], square[pl.ds(1, half, stride=2), :]
        ) * scale
        zbuf[r, z] = jnp.where(lax.rem(n, slots) < sizes[pipe], out, 0.0).astype(jnp.bfloat16)
        for o in far_first(n_z):
            z_copy(r, o).start()

    def finish(r):
        for o in range(1, n_z):
            z_copy(r, o).wait_recv()
        total = zbuf[r, 0].astype(jnp.float32)
        for zz in range(1, n_z):
            total = total + zbuf[r, zz].astype(jnp.float32)
        sk[r * ring + me] = total.astype(jnp.bfloat16)
        for o in far_first(ring):
            x_copy(r, o).start()

    mix_load.wait()
    acts_load(0).wait()

    def start_slopes(q):
        for h in group(q):
            for k in range(slots):
                slopes(0, k, h)

    start_slopes(0)
    sizes_load.wait()

    @pl.when(jnp.logical_and(pipe > 0, pipe < n_pipe - 1))
    def _():
        pl.semaphore_wait(barrier, 6)

    @pl.when(jnp.logical_or(pipe == 0, pipe == n_pipe - 1))
    def _():
        pl.semaphore_wait(barrier, 5)

    tell(0)

    @pl.when(jnp.logical_not(top))
    def _():
        tiles_load.wait()
        blocks_load.wait()
        for q in range(GROUPS):
            build(q)
        hear(0)
        tell(1)
        for q in range(1, GROUPS):
            start_slopes(q)
        hear(1)
        tell(2)

    def step(m, c):
        after = jnp.minimum(m + 1, micro - 1)

        @pl.when(top)
        def _():
            grad_load(m).wait()

        @pl.when(m + 1 < micro)
        def _():
            acts_load(after).wait()

        for q in range(GROUPS):
            @pl.when(jnp.logical_not(top))
            def _():
                relay(m, q).wait_recv()

            chain(m, q, after)

            @pl.when(pipe > 0)
            def _():
                relay(m, q).start()

            if q == 0:
                @pl.when(m == 1)
                def _():
                    hear(2)

                @pl.when(m > 0)
                def _():
                    send_parts(m - 1)

            @pl.when(jnp.logical_and(m == 0, top))
            def _():
                if q == 0:
                    tiles_load.wait()
                    blocks_load.wait()
                build(q)
                if q + 1 < GROUPS:
                    start_slopes(q + 1)
                if q == 0:
                    hear(0)
                    tell(1)
                if q == GROUPS - 1:
                    hear(1)
                    tell(2)

        for r in range(rounds - 1):
            @pl.when(m == (ring * (r + 1) - 1) // slots + 2)
            def _():
                outer(r)

        for r in range(rounds - 2):
            @pl.when(m == (ring * (r + 1) - 1) // slots + 4)
            def _():
                finish(r)

        return c

    lax.fori_loop(0, micro, step, 0)
    for k in range(slots - 1, -1, -1):
        project(micro - 1, GROUPS - 1, k)
    send_parts(micro - 1)
    outer(rounds - 1)

    def drain(m, c):
        @pl.when(pipe > 0)
        def _():
            for q in range(GROUPS):
                relay(m, q).wait_send()

        for k in range(slots):
            owner, copy = part_copy(m, k)

            @pl.when(owner != me)
            def _():
                copy.wait_send()

        return c

    lax.fori_loop(0, micro, drain, 0)
    def unpack(r):
        for o in range(1, ring):
            x_copy(r, o).wait_recv()
        for n in range(r * ring, (r + 1) * ring):
            m, k = divmod(n, slots)
            rows = pl.ds(k * half * micro + m, half, stride=micro)
            sk_out[rows, :] = sk[n].astype(jnp.float32)

    finish(rounds - 2)
    for r in range(rounds - 2):
        unpack(r)
    for r in range(rounds):
        for o in range(1, n_z):
            z_copy(r, o).wait_send()
    finish(rounds - 1)
    for r in range(rounds - 2, rounds):
        unpack(r)
    for r in range(rounds):
        for o in range(1, ring):
            x_copy(r, o).wait_send()


def shards(n_dp, n_pipe, n_tensor, grad_out, activations, mixing, proj_tiles, proj_blocks, section_sizes):
    micro, tokens, width = grad_out.shape
    slots = activations.shape[1]
    heads, hs = mixing.shape[2:4]
    n_tiles = proj_tiles.shape[2]
    rank = proj_tiles.shape[4] // 2
    units = micro * slots
    ring = 2 * n_tensor
    rounds = units // ring
    n_z = n_dp // 2
    bf16, f32 = jnp.bfloat16, jnp.float32
    hbm = pl.BlockSpec(memory_space=pltpu.HBM)
    vmem = pl.BlockSpec(memory_space=pltpu.VMEM)
    dma = pltpu.SemaphoreType.DMA
    gout, sk = pl.pallas_call(
        functools.partial(kernel, n_dp, n_pipe, n_tensor, 1.0 / math.sqrt(tokens * n_dp)),
        out_shape=(
            pltpu.VMEM((micro, tokens, width), bf16),
            pltpu.VMEM((units * rank // 2, 2 * rank), f32),
        ),
        in_specs=[hbm] * 6,
        out_specs=(vmem, vmem),
        scratch_shapes=[
            pltpu.SMEM(section_sizes.shape, jnp.int32),
            pltpu.SMEM((slots, 1, n_tiles), jnp.int32),
            pltpu.VMEM((slots, micro, tokens, width), bf16),
            pltpu.VMEM((micro, tokens, width), bf16),
            pltpu.VMEM((slots, heads, hs, hs), bf16),
            pltpu.VMEM((slots, n_tiles, hs, 2 * rank), bf16),
            pltpu.VMEM((slots, width, 2 * rank), bf16),
            pltpu.VMEM((slots, tokens, width), f32),
            pltpu.VMEM((slots, tokens, width), bf16),
            pltpu.VMEM((slots, tokens, 2 * rank), f32),
            pltpu.VMEM((units, tokens, 2 * rank), bf16),
            pltpu.VMEM((rounds, ring - 1, tokens, 2 * rank), bf16),
            pltpu.VMEM((rounds, n_z, rank // 2, 2 * rank), bf16),
            pltpu.VMEM((units, rank // 2, 2 * rank), bf16),
            pltpu.VMEM((rank, 2 * rank), f32),
            dma((micro,)), dma((micro,)), dma((4,)),
            pltpu.SemaphoreType.REGULAR((3,)), pltpu.SemaphoreType.REGULAR((3,)),
            dma((micro, GROUPS)), dma((micro, GROUPS)),
            dma((units,)), dma((rounds, ring - 1)),
            dma((rounds, n_z - 1)), dma((rounds, n_z - 1)),
            dma((rounds, ring - 1)), dma((rounds, ring - 1)),
        ],
        compiler_params=pltpu.CompilerParams(
            collective_id=0, has_side_effects=True, vmem_limit_bytes=40 << 20
        ),
    )(*[
        pltpu.with_memory_space_constraint(x, pltpu.HBM)
        for x in (section_sizes, proj_blocks.transpose(1, 0, 2), grad_out, activations, mixing, proj_tiles)
    ])
    grads, sk = pl.pallas_call(
        store,
        out_shape=(
            jax.ShapeDtypeStruct((1,) + gout.shape, bf16), jax.ShapeDtypeStruct(sk.shape, f32),
        ),
        in_specs=[vmem, vmem],
        out_specs=(hbm, hbm),
        scratch_shapes=[dma((2,))],
        compiler_params=pltpu.CompilerParams(vmem_limit_bytes=1 << 20),
    )(*[pltpu.with_memory_space_constraint(x, pltpu.VMEM) for x in (gout, sk)])
    sk = sk.reshape(slots, rank // 2, micro, 2 * rank).transpose(0, 2, 1, 3)
    return grads, sk.reshape(1, slots, micro, rank * rank)


def solution(mesh):
    return jax.shard_map(
        functools.partial(shards, mesh.shape["dp"], mesh.shape["pipe"], mesh.shape["tensor"]),
        mesh=mesh,
        in_specs=(
            P(None, "dp", "tensor"),
            P("pipe", None, None, "dp", "tensor"),
            P("pipe", None, "tensor", None, None),
            P("pipe", None, None, None, None),
            P("pipe", None, None),
            P(),
        ),
        out_specs=(P("pipe", None, "dp", "tensor"), P("pipe", None, None, None)),
        check_vma=False,
    )
```
